256 devices in a mesh: oct: 16 (over y, x), cube: 16 (over z, core).
Axes of the slice: x: 4, y: 4, z: 8, core: 2. Of those that a mesh axis runs over, the one named last changes fastest.
Arguments:
- charges: bfloat16 [65536, 128], P(('oct', 'cube')), may hold values from -6 to 6
- panel_counts: int32 [65536], P(('oct', 'cube')), may hold values from 32 to 128
- positions: float32 [3, 65536, 128], P(None, ('oct', 'cube')), may hold values from 0 to 2
- moment_map: bfloat16 [128, 128], replicated, may hold values from -0.5 to 0.5
- translations: bfloat16 [16, 128, 128], replicated, may hold values from -0.15625 to 0.15625
- evaluation: bfloat16 [128, 128], replicated, may hold values from -0.5 to 0.5
- near_boxes: int32 [65536, 4], P(('oct', 'cube')), may hold values from 0 to 255
- group_sources: int32 [65536, 8], P(('oct', 'cube')), may hold values from 0 to 4095
- group_patterns: int32 [65536, 8], P(('oct', 'cube')), may hold values from 0 to 15
- remote_sources: int32 [16, 16, 16, 64, 4], P('oct', 'cube'), may hold values from 0 to 255
- remote_patterns: int32 [16, 16, 16, 64, 4], P('oct', 'cube'), may hold values from 0 to 15
- remote_targets: int32 [16, 16, 16, 64], P('oct', 'cube'), may hold values from 0 to 255
Outputs:
- potential: float32 [65536, 128], P(('oct', 'cube'))
The draws below stay inside these ranges and needn't reach their ends.
All inputs are finite; a program needn't handle non-finite values.
Results may differ from the reference program's by a relative error of at most 0.0024.
Values may be sent and summed in bfloat16 or wider, within the bound.
A program may use at most 64 MiB of HBM per device.

```python
import math
import jax
import jax.numpy as jnp
from jax import lax

BOX_DEV = 256
NPAN = 128
COEFF = 128
NPAT = 16
KNEAR = 4
KLIST = 8
SLOTS = 64
KREMOTE = 4
NBOX = 65536
GROUP = 4096
N_OCT = 16
N_CUBE = 16


def touch_ends(array, stream_key, smallest, largest):
    shape = array.shape
    place = [jax.random.randint(jax.random.fold_in(stream_key, axis), (), 0, shape[axis]) for axis in range(len(shape))]
    array = array.at[tuple(place)].set(smallest)
    longest = shape.index(max(shape))
    place[longest] = (place[longest] + 1) % shape[longest]
    return array.at[tuple(place)].set(largest)


def block_levels(own_key, dims, pieces, low, top_value):
    loudness, own = 1.0, jax.random.fold_in(own_key, 6)
    for dim, parts in pieces:
        draws = jnp.exp(jax.random.uniform(jax.random.fold_in(own, dim), (parts,), jnp.float32, low / len(pieces), top_value / len(pieces)))
        loudness = loudness * jnp.repeat(draws, dims[dim] // parts).reshape([-1 if axis == dim else 1 for axis in range(len(dims))])
    return loudness


def centred(stream_key, extent, scale, most, pieces=(), kind=jnp.bfloat16):
    drawn = jax.random.normal(stream_key, extent, jnp.float32) * scale
    if len(pieces) > 0:
        drawn = block_levels(stream_key, extent, pieces, -0.22, 0.18) * drawn
    return jnp.clip(drawn, min=-most, max=most).astype(kind)


def setup_inputs(seed: int = 0) -> dict:
    arg_keys = jax.random.split(jax.random.key(seed), 13)
    charges = centred(arg_keys[0], (NBOX, NPAN), 1.0, 6.0, ((0, 256),))
    panel_counts = touch_ends(jax.random.randint(arg_keys[1], (NBOX,), NPAN // 4, NPAN + 1), jax.random.fold_in(arg_keys[1], 1), NPAN // 4, NPAN).astype(jnp.int32)
    positions = jnp.clip(2.0 * jax.random.uniform(arg_keys[2], (3, NBOX, NPAN), jnp.float32) ** block_levels(arg_keys[2], (3, NBOX, NPAN), ((1, 256),), -0.2, 0.2), 0.0, 2.0)
    moment_map = centred(arg_keys[3], (NPAN, COEFF), NPAN ** -0.5, 0.5)
    translations = centred(arg_keys[4], (NPAT, COEFF, COEFF), (COEFF * (KLIST + KREMOTE)) ** -0.5, 0.15625)
    evaluation = centred(arg_keys[5], (COEFF, NPAN), COEFF ** -0.5, 0.5)
    near_boxes = touch_ends(jax.random.randint(arg_keys[6], (NBOX, KNEAR), 0, BOX_DEV), jax.random.fold_in(arg_keys[6], 1), 0, BOX_DEV - 1).astype(jnp.int32)
    group_sources = touch_ends(jax.random.randint(arg_keys[7], (NBOX, KLIST), 0, GROUP), jax.random.fold_in(arg_keys[7], 1), 0, GROUP - 1).astype(jnp.int32)
    group_patterns = touch_ends(jax.random.randint(arg_keys[8], (NBOX, KLIST), 0, NPAT), jax.random.fold_in(arg_keys[8], 1), 0, NPAT - 1).astype(jnp.int32)
    remote_sources = touch_ends(jax.random.randint(arg_keys[9], (N_OCT, N_CUBE, N_OCT, SLOTS, KREMOTE), 0, BOX_DEV), jax.random.fold_in(arg_keys[9], 1), 0, BOX_DEV - 1).astype(jnp.int32)
    remote_patterns = touch_ends(jax.random.randint(arg_keys[10], (N_OCT, N_CUBE, N_OCT, SLOTS, KREMOTE), 0, NPAT), jax.random.fold_in(arg_keys[10], 1), 0, NPAT - 1).astype(jnp.int32)
    remote_targets = touch_ends(jax.random.randint(arg_keys[11], (N_OCT, N_CUBE, N_OCT, SLOTS), 0, BOX_DEV), jax.random.fold_in(arg_keys[11], 1), 0, BOX_DEV - 1).astype(jnp.int32)
    return {"charges": charges, "panel_counts": panel_counts, "positions": positions, "moment_map": moment_map, "translations": translations, "evaluation": evaluation, "near_boxes": near_boxes, "group_sources": group_sources, "group_patterns": group_patterns, "remote_sources": remote_sources, "remote_patterns": remote_patterns, "remote_targets": remote_targets}


def pattern_sums(rows, patterns):
    onehot = (patterns[..., None] == jnp.arange(NPAT, dtype=jnp.int32)).astype(jnp.float32)
    summed = jnp.einsum('nkp,nkc->npc', onehot, rows.astype(jnp.float32))
    return summed.astype(jnp.bfloat16).reshape(rows.shape[0], NPAT * COEFF)

def near_block(args):
    target_pos, source_pos, source_q = args
    diffs = target_pos[:, :, None, :, None] - source_pos[:, :, :, None, :]
    dist_sq = lax.optimization_barrier(jnp.sum(diffs * diffs, axis=0)) + 0.0025
    kernel = source_q[:, :, None, :] * lax.rsqrt(dist_sq)
    return lax.optimization_barrier(jnp.sum(kernel, axis=(1, 3)))

def reference(charges, panel_counts, positions, moment_map, translations, evaluation, near_boxes, group_sources, group_patterns, remote_sources, remote_patterns, remote_targets):
    slot_index = jnp.arange(NPAN, dtype=jnp.int32)
    live = slot_index[None, :] < panel_counts[:, None]
    strength = jnp.where(live, charges, jnp.zeros_like(charges))
    multipole = jnp.dot(strength, moment_map, preferred_element_type=jnp.float32).astype(jnp.bfloat16)
    operators = translations.reshape(NPAT * COEFF, COEFF)
    box_ids = jnp.arange(NBOX, dtype=jnp.int32)
    group_base = box_ids // GROUP * GROUP
    group_rows = multipole[(group_base[:, None] + group_sources).astype(jnp.int32)]
    group_sum = pattern_sums(group_rows, group_patterns)
    near_local = jnp.dot(group_sum, operators, preferred_element_type=jnp.float32)

    def per_sender(args):
        octant, sources, patterns = args
        cube_ids = jnp.arange(N_CUBE, dtype=jnp.int32)
        base = (octant * N_CUBE + cube_ids) * BOX_DEV
        index = (base[:, None, None, None] + sources).astype(jnp.int32)
        rows = multipole[index].reshape(-1, KREMOTE, COEFF)
        slot_sum = pattern_sums(rows, patterns.reshape(-1, KREMOTE))
        return jnp.dot(slot_sum, operators, preferred_element_type=jnp.float32)
    octants = jnp.arange(N_OCT, dtype=jnp.int32)
    slot_local = lax.map(per_sender, (octants, remote_sources, remote_patterns))
    slot_local = slot_local.reshape(-1, COEFF)
    dest = jnp.arange(N_OCT, dtype=jnp.int32)[None, None, :, None]
    cube = jnp.arange(N_CUBE, dtype=jnp.int32)[None, :, None, None]
    target = ((dest * N_CUBE + cube) * BOX_DEV + remote_targets).reshape(-1).astype(jnp.int32)
    remote_local = jnp.zeros((NBOX, COEFF), jnp.float32).at[target].add(slot_local)
    local = (near_local + remote_local).astype(jnp.bfloat16)
    far = jnp.dot(local, evaluation, preferred_element_type=jnp.float32)
    device_base = box_ids // BOX_DEV * BOX_DEV
    near_index = (device_base[:, None] + near_boxes).astype(jnp.int32)
    strength_f = strength.astype(jnp.float32)
    block = 64
    count = NBOX // block if NBOX % block == 0 else NBOX
    size = NBOX // count
    target_pos = positions.reshape(3, count, size, NPAN).transpose(1, 0, 2, 3)
    source_pos = positions[:, near_index].reshape(3, count, size, KNEAR, NPAN).transpose(1, 0, 2, 3, 4)
    source_q = strength_f[near_index].reshape(count, size, KNEAR, NPAN)
    near = lax.map(near_block, (target_pos, source_pos, source_q)).reshape(NBOX, NPAN)
    total = near * (1.0 / (4.0 * math.pi)) + far
    return jnp.where(live, total, jnp.zeros_like(total))
```

```python
import functools
import math

import jax
import jax.numpy as jnp
from jax import lax
from jax.experimental import pallas as pl
from jax.experimental.pallas import tpu as pltpu
from jax.sharding import PartitionSpec as P

F32, BF16, I32 = jnp.float32, jnp.bfloat16, jnp.int32
MESH = pl.DeviceIdType.MESH
FEAT = 32
SOFT = 0.0025
NEAR_UNROLL = 32


def parts3(v):
    hi = v.astype(BF16).astype(F32)
    rest = v - hi
    mid = rest.astype(BF16).astype(F32)
    return hi, mid, rest - mid


def merge(a, b, first, shift, axis):
    return jnp.where(first, a, b) + pltpu.roll(jnp.where(first, b, a), shift, axis)


def column(row):
    return jnp.broadcast_to(row, (128, 128)).T


def build_features(p_ref, src_b, tgt_b, sub, unroll):
    is3, is7, lo3, lo4 = sub == 3, sub == 7, sub < 3, sub < 4
    pad = is3 | is7
    zero = jnp.zeros((8, 128), F32)

    def some(ii, carry):
        for bu in range(unroll):
            i = ii * unroll + bu
            cols = []
            for u in range(4):
                t = 4 * i + u
                v = jnp.where(pad, 0.0, p_ref[t] - 1.0)
                s = v * v
                s = s + pltpu.roll(s, 1, 0)
                n = s + pltpu.roll(s, 2, 0)
                w1, w2, w3 = parts3(jnp.where(pad, n, v))
                s0 = jnp.where(is7, 1.0, w1)
                s1 = jnp.where(is7, 1.0, w2)
                s2 = jnp.where(is7, 1.0, jnp.where(lo3, w1, w3))
                src_b[t] = jnp.concatenate([s0, s1, s2, zero], axis=0).astype(BF16)
                m1, m2, m3 = parts3(n + SOFT)
                y1, y2, y3 = -2.0 * w1, -2.0 * w2, -2.0 * w3
                base = jnp.where(is3, 1.0, jnp.where(lo4, y1, y2))
                t0 = jnp.where(is7, m1, base)
                t1 = jnp.where(is7, m2, base)
                t2 = jnp.where(is7, m3, jnp.where(is3, 1.0, jnp.where(lo4, y3, y1)))
                cols += [t0, t1, t2, zero]
            tgt_b[i] = jnp.concatenate(cols, axis=0).T.astype(BF16)
        return carry

    lax.fori_loop(0, src_b.shape[0] // (4 * unroll), some, 0)


def near_boxes_step(i, nb_ref, q_ref, src_b, tgt_b, near_ref, lane, sub):
    t0 = pl.multiple_of(NEAR_UNROLL * i, NEAR_UNROLL)
    knear = nb_ref.shape[0]
    rows = []
    for u in range(NEAR_UNROLL):
        lhs = tgt_b[(NEAR_UNROLL // 4) * i + u // 4]
        lo = FEAT * (u % 4)
        acc = None
        for pair in range(knear // 2):
            ids = [nb_ref[2 * pair + e, t0 + u] for e in range(2)]
            parts = [jnp.concatenate([src_b[s] for s in ids], axis=1)]
            if lo:
                parts.insert(0, jnp.zeros((lo, 256), BF16))
            if lo + FEAT < 128:
                parts.append(jnp.zeros((128 - FEAT - lo, 256), BF16))
            rhs = jnp.concatenate(parts, axis=0)
            inv = lax.rsqrt(jnp.dot(lhs, rhs, preferred_element_type=F32))
            for e in range(2):
                q = q_ref[pl.ds(ids[e], 1), :]
                term = inv[:, 128 * e : 128 * e + 128] * q
                acc = term if acc is None else acc + term
        row = None
        for g in range(16):
            total = jnp.sum(acc[8 * g : 8 * g + 8], axis=1, keepdims=True)
            x = jnp.where(lane == sub + 8 * g, total, 0.0)
            row = x if row is None else row + x
        rows.append(row)
    for b in range(NEAR_UNROLL // 8):
        some = rows[8 * b : 8 * b + 8]
        shift = 1
        while len(some) > 1:
            first = (sub & shift) == 0
            some = [merge(some[2 * n], some[2 * n + 1], first, shift, 0) for n in range(len(some) // 2)]
            shift *= 2
        near_ref[pl.ds(t0 + 8 * b, 8), :] = some[0]


def step_kernel(
    n_oct,
    n_cube,
    nb_ref,
    gs_ref,
    pos_ref,
    charges_ref,
    counts_ref,
    moment_ref,
    trans_ref,
    eval_ref,
    gp_ref,
    rs_ref,
    rp_ref,
    rt_ref,
    out_ref,
    p_ref,
    src_b,
    tgt_b,
    q_ref,
    near_ref,
    count_b,
    pat_b,
    gall,
    gf_ref,
    table,
    key_v,
    key_s,
    slot_f,
    msg,
    got,
    rows_ref,
    sums_ref,
    pos_sem,
    key_sem,
    right_send,
    right_recv,
    left_send,
    left_recv,
    sib_send,
    sib_recv,
    oct_send,
    oct_recv,
):
    o = lax.axis_index("oct")
    c = lax.axis_index("cube")
    boxes, panels = charges_ref.shape
    width = moment_ref.shape[1]
    n_pat = trans_ref.shape[0]
    klist = gs_ref.shape[0]
    fanin = rs_ref.shape[1]
    slots = rs_ref.shape[2]
    chips = n_cube // 2
    right = lax.rem(c + 2, n_cube)
    left = lax.rem(c + n_cube - 2, n_cube)
    sib = c + 1 - 2 * lax.rem(c, 2)

    barrier = pltpu.get_barrier_semaphore()
    for peer in (right, left, sib):
        pl.semaphore_signal(barrier, inc=1, device_id={"cube": peer}, device_id_type=MESH)
    for i in range(n_oct - 1):
        d = lax.rem(o + 1 + i, n_oct)
        pl.semaphore_signal(barrier, inc=1, device_id={"oct": d}, device_id_type=MESH)

    pos_copies = [
        pltpu.make_async_copy(pos_ref.at[d], p_ref.at[:, d + 4 * e], pos_sem.at[d + 3 * e])
        for d in range(3)
        for e in range(2)
    ]
    for copy in pos_copies:
        copy.start()

    key_v[...] = rp_ref[...] * boxes + rs_ref[...]
    key_copy = pltpu.make_async_copy(key_v, key_s, key_sem.at[0])
    key_copy.start()

    lane = lax.broadcasted_iota(I32, (8, 128), 1)
    sub = lax.broadcasted_iota(I32, (8, 128), 0)

    lane_big = lax.broadcasted_iota(I32, (128, 128), 1)
    for h in range(boxes // 128):
        half = slice(128 * h, 128 * h + 128)
        count_b[half] = column(counts_ref[h : h + 1, :])
        charge = charges_ref[half].astype(F32)
        q_ref[half] = jnp.where(lane_big < count_b[half], charge, 0.0)
    strength = q_ref[...].astype(BF16)
    multipole = jnp.dot(strength, moment_ref[...], preferred_element_type=F32).astype(BF16)
    gall[c] = multipole
    for p in range(n_pat):
        table[p * boxes : (p + 1) * boxes] = jnp.dot(
            multipole, trans_ref[p], preferred_element_type=F32
        )

    pl.semaphore_wait(barrier, 3 + n_oct - 1)

    def send(shard, peer, sends, recvs, n):
        return pltpu.make_async_remote_copy(
            src_ref=gall.at[shard],
            dst_ref=gall.at[shard],
            send_sem=sends.at[n],
            recv_sem=recvs.at[n],
            device_id={"cube": peer},
            device_id_type=MESH,
        )

    n_right = chips // 2
    n_left = chips - 1 - n_right
    from_left = [lax.rem(c + n_cube - 2 * h, n_cube) for h in range(n_right + 1)]
    from_right = [lax.rem(c + 2 * h, n_cube) for h in range(n_left + 1)]
    to_right = [send(from_left[h], right, right_send, right_recv, h) for h in range(n_right)]
    to_left = [send(from_right[h], left, left_send, left_recv, h) for h in range(n_left)]
    to_sib = [send(from_left[h], sib, sib_send, sib_recv, h) for h in range(n_right + 1)]
    to_sib += [
        send(from_right[h], sib, sib_send, sib_recv, n_right + h) for h in range(1, n_left + 1)
    ]

    to_right[0].start()
    to_left[0].start()
    to_sib[0].start()

    def ring_step(h):
        if h <= n_right:
            to_right[h - 1].wait_recv()
        if h <= n_left:
            to_left[h - 1].wait_recv()
        if h < n_right:
            to_right[h].start()
        if h < n_left:
            to_left[h].start()
        if h <= n_right:
            to_sib[h].start()
        if h <= n_left:
            to_sib[n_right + h].start()

    key_copy.wait()
    targets = rt_ref[...].astype(F32)
    blank = jnp.zeros_like(targets)
    odd = lax.rem(o, 2)
    target_rows = jnp.where(
        odd == 0,
        jnp.concatenate([targets, blank], axis=1),
        jnp.concatenate([blank, targets], axis=1),
    )
    for d in range(n_oct):
        msg[d, slots : slots + 16, :] = jnp.broadcast_to(
            target_rows[d : d + 1], (16, 2 * slots)
        ).astype(BF16)

    def fill(d):
        for j in range(slots):
            total = None
            for k in range(fanin):
                row = table[pl.ds(key_s[d, k, j], 1), :]
                total = row if total is None else total + row
            slot_f[j : j + 1, :] = total
        msg[d, 0:slots, :] = slot_f[...].astype(BF16)

    def to_oct(i):
        d = lax.rem(o + 1 + i, n_oct)
        return pltpu.make_async_remote_copy(
            src_ref=msg.at[d],
            dst_ref=got.at[o],
            send_sem=oct_send.at[i],
            recv_sem=oct_recv.at[i],
            device_id={"oct": d},
            device_id_type=MESH,
        )

    def one_group(i, carry):
        fill(lax.rem(o + 1 + i, n_oct))

        @pl.when(i < n_oct - 1)
        def _():
            to_oct(i).start()

        return carry

    lax.fori_loop(0, n_oct, one_group, 0)
    got[o] = msg[o]

    for copy in pos_copies:
        copy.wait()
    build_features(p_ref, src_b, tgt_b, sub, 8)
    for k in range(klist):
        for h in range(boxes // 128):
            pat_b[k, 128 * h : 128 * h + 128] = column(gp_ref[k : k + 1, 128 * h : 128 * h + 128])

    def near_step(i, carry):
        for h in range(1, n_right + 1):

            @pl.when(i == h)
            def _(h=h):
                ring_step(h)

        near_boxes_step(i, nb_ref, q_ref, src_b, tgt_b, near_ref, lane, sub)
        return carry

    lax.fori_loop(0, boxes // NEAR_UNROLL, near_step, 0)

    for copy in to_sib:
        copy.wait_recv()
    gf_ref[...] = gall[...].reshape(n_cube * boxes, width).astype(F32)

    def gather(i, carry):
        t0 = pl.multiple_of(16 * i, 16)
        for u in range(16):
            for k in range(klist):
                rows_ref[k, pl.ds(t0 + u, 1), :] = gf_ref[pl.ds(gs_ref[k, t0 + u], 1), :]
        return carry

    lax.fori_loop(0, boxes // 16, gather, 0)

    def pattern_sums(i, carry):
        t0 = pl.ds(pl.multiple_of(16 * i, 16), 16)
        pats = [pat_b[k, t0] for k in range(klist)]
        rows = [rows_ref[k, t0] for k in range(klist)]
        for p in range(n_pat):
            total = None
            for k in range(klist):
                x = jnp.where(pats[k] == p, rows[k], 0.0)
                total = x if total is None else total + x
            sums_ref[t0, p * width : (p + 1) * width] = total.astype(BF16)
        return carry

    lax.fori_loop(0, boxes // 16, pattern_sums, 0)
    operators = trans_ref[...].reshape(n_pat * width, width)
    local = jnp.dot(sums_ref[...], operators, preferred_element_type=F32)

    for i in range(n_oct - 1):
        to_oct(i).wait_recv()
    box = lax.broadcasted_iota(I32, (boxes, 2 * slots), 0).astype(F32)
    for m in range(n_oct // 4):
        hot, vals = [], []
        for e in (4 * m, 4 * m + 2):
            trow = got[e, slots : slots + 16, :].astype(F32) + got[
                e + 1, slots : slots + 16, :
            ].astype(F32)
            hot.append(jnp.where(box == trow[0:1], 1.0, 0.0).astype(BF16))
            vals += [got[e, 0:slots, :], got[e + 1, 0:slots, :]]
        local = local + jnp.dot(
            jnp.concatenate(hot, axis=1),
            jnp.concatenate(vals, axis=0),
            preferred_element_type=F32,
        )

    far = jnp.dot(local.astype(BF16), eval_ref[...], preferred_element_type=F32)
    total = near_ref[...] * (1.0 / (4.0 * math.pi)) + far
    panel = lax.broadcasted_iota(I32, (boxes, panels), 1)
    out_ref[...] = jnp.where(panel < count_b[...], total, 0.0)

    for copy in to_right + to_left + to_sib:
        copy.wait_send()
    for i in range(n_oct - 1):
        to_oct(i).wait_send()


def body(
    n_oct,
    n_cube,
    charges,
    panel_counts,
    positions,
    moment_map,
    translations,
    evaluation,
    near_boxes,
    group_sources,
    group_patterns,
    remote_sources,
    remote_patterns,
    remote_targets,
):
    boxes, panels = charges.shape
    width = moment_map.shape[1]
    n_pat = translations.shape[0]
    klist = group_sources.shape[1]
    slots, fanin = remote_sources.shape[3:]
    chips = n_cube // 2
    sources = remote_sources[0, 0].transpose(0, 2, 1)
    patterns = remote_patterns[0, 0].transpose(0, 2, 1)
    smem = pl.BlockSpec(memory_space=pltpu.SMEM)
    vmem = pl.BlockSpec(memory_space=pltpu.VMEM)
    dma = pltpu.SemaphoreType.DMA
    return pl.pallas_call(
        functools.partial(step_kernel, n_oct, n_cube),
        out_shape=jax.ShapeDtypeStruct((boxes, panels), F32),
        in_specs=[smem, smem, pl.BlockSpec(memory_space=pl.ANY)] + [vmem] * 9,
        out_specs=vmem,
        scratch_shapes=[
            pltpu.VMEM((boxes, 8, panels), F32),
            pltpu.VMEM((boxes, FEAT, panels), BF16),
            pltpu.VMEM((boxes // 4, panels, 4 * FEAT), BF16),
            pltpu.VMEM((boxes, panels), F32),
            pltpu.VMEM((boxes, panels), F32),
            pltpu.VMEM((boxes, panels), I32),
            pltpu.VMEM((klist, boxes, width), I32),
            pltpu.VMEM((n_cube, boxes, width), BF16),
            pltpu.VMEM((n_cube * boxes, width), F32),
            pltpu.VMEM((n_pat * boxes, width), F32),
            pltpu.VMEM((n_oct, fanin, slots), I32),
            pltpu.SMEM((n_oct, fanin, slots), I32),
            pltpu.VMEM((slots, width), F32),
            pltpu.VMEM((n_oct, slots + 16, width), BF16),
            pltpu.VMEM((n_oct, slots + 16, width), BF16),
            pltpu.VMEM((klist, boxes, width), F32),
            pltpu.VMEM((boxes, n_pat * width), BF16),
            dma((6,)),
            dma((1,)),
            dma((chips,)),
            dma((chips,)),
            dma((chips,)),
            dma((chips,)),
            dma((chips,)),
            dma((chips,)),
            dma((n_oct,)),
            dma((n_oct,)),
        ],
        compiler_params=pltpu.CompilerParams(
            collective_id=0, has_side_effects=True, vmem_limit_bytes=48 << 20
        ),
    )(
        near_boxes.T,
        group_sources.T,
        positions,
        charges,
        panel_counts.reshape(boxes // 128, 128),
        moment_map,
        translations,
        evaluation,
        group_patterns.T,
        sources,
        patterns,
        remote_targets[0, 0],
    )


def solution(mesh):
    n_oct, n_cube = mesh.shape["oct"], mesh.shape["cube"]
    return jax.shard_map(
        functools.partial(body, n_oct, n_cube),
        mesh=mesh,
        in_specs=(
            P(("oct", "cube"), None),
            P(("oct", "cube")),
            P(None, ("oct", "cube"), None),
            P(),
            P(),
            P(),
            P(("oct", "cube"), None),
            P(("oct", "cube"), None),
            P(("oct", "cube"), None),
            P("oct", "cube", None, None, None),
            P("oct", "cube", None, None, None),
            P("oct", "cube", None, None),
        ),
        out_specs=P(("oct", "cube"), None),
        check_vma=False,
    )
```

```python
import functools
import math

import jax
import jax.numpy as jnp
from jax import lax
from jax.experimental import pallas as pl
from jax.experimental.pallas import tpu as pltpu
from jax.sharding import PartitionSpec as P

F32, BF16, I32 = jnp.float32, jnp.bfloat16, jnp.int32
MESH = pl.DeviceIdType.MESH
FEAT = 32
SOFT = 0.0025
NEAR_UNROLL = 32
RING_FROM = 2


def parts3(v):
    hi = v.astype(BF16).astype(F32)
    rest = v - hi
    mid = rest.astype(BF16).astype(F32)
    return hi, mid, rest - mid


def merge(a, b, first, shift, axis):
    return jnp.where(first, a, b) + pltpu.roll(jnp.where(first, b, a), shift, axis)


def column(row):
    return jnp.broadcast_to(row, (128, 128)).T


def features_of_four(i, p_ref, src_b, tgt_b, sub):
    is3, is7, lo3, lo4 = sub == 3, sub == 7, sub < 3, sub < 4
    pad = is3 | is7
    zero = jnp.zeros((8, 128), F32)
    cols = []
    for u in range(4):
        t = 4 * i + u
        v = jnp.where(pad, 0.0, p_ref[t] - 1.0)
        s = v * v
        s = s + pltpu.roll(s, 1, 0)
        n = s + pltpu.roll(s, 2, 0)
        w1, w2, w3 = parts3(jnp.where(pad, n, v))
        s0 = jnp.where(is7, 1.0, w1)
        s1 = jnp.where(is7, 1.0, w2)
        s2 = jnp.where(is7, 1.0, jnp.where(lo3, w1, w3))
        src_b[t] = jnp.concatenate([s0, s1, s2, zero], axis=0).astype(BF16)
        m1, m2, m3 = parts3(n + SOFT)
        y1, y2, y3 = -2.0 * w1, -2.0 * w2, -2.0 * w3
        base = jnp.where(is3, 1.0, jnp.where(lo4, y1, y2))
        t0 = jnp.where(is7, m1, base)
        t1 = jnp.where(is7, m2, base)
        t2 = jnp.where(is7, m3, jnp.where(is3, 1.0, jnp.where(lo4, y3, y1)))
        cols += [t0, t1, t2, zero]
    tgt_b[i] = jnp.concatenate(cols, axis=0).T.astype(BF16)


def near_boxes_step(i, nb_ref, q_ref, src_b, tgt_b, near_ref, lane, sub):
    t0 = pl.multiple_of(NEAR_UNROLL * i, NEAR_UNROLL)
    knear = nb_ref.shape[0]
    rows = []
    for u in range(NEAR_UNROLL):
        lhs = tgt_b[(NEAR_UNROLL // 4) * i + u // 4]
        lo = FEAT * (u % 4)
        acc = None
        for pair in range(knear // 2):
            ids = [nb_ref[2 * pair + e, t0 + u] for e in range(2)]
            parts = [jnp.concatenate([src_b[s] for s in ids], axis=1)]
            if lo:
                parts.insert(0, jnp.zeros((lo, 256), BF16))
            if lo + FEAT < 128:
                parts.append(jnp.zeros((128 - FEAT - lo, 256), BF16))
            rhs = jnp.concatenate(parts, axis=0)
            inv = lax.rsqrt(jnp.dot(lhs, rhs, preferred_element_type=F32))
            for e in range(2):
                q = q_ref[pl.ds(ids[e], 1), :]
                term = inv[:, 128 * e : 128 * e + 128] * q
                acc = term if acc is None else acc + term
        row = None
        for g in range(16):
            total = jnp.sum(acc[8 * g : 8 * g + 8], axis=1, keepdims=True)
            x = jnp.where(lane == sub + 8 * g, total, 0.0)
            row = x if row is None else row + x
        rows.append(row)
    for b in range(NEAR_UNROLL // 8):
        some = rows[8 * b : 8 * b + 8]
        shift = 1
        while len(some) > 1:
            first = (sub & shift) == 0
            some = [merge(some[2 * n], some[2 * n + 1], first, shift, 0) for n in range(len(some) // 2)]
            shift *= 2
        near_ref[pl.ds(t0 + 8 * b, 8), :] = some[0]


def step_kernel(
    n_oct,
    n_cube,
    pos_ref,
    charges_in,
    counts_in,
    moment_in,
    trans_in,
    rs_in,
    rp_in,
    nb_in,
    rt_in,
    gs_in,
    gp_in,
    eval_in,
    out_ref,
    charges_ref,
    counts_ref,
    moment_ref,
    trans_ref,
    rs_ref,
    rp_ref,
    nb_ref,
    rt_ref,
    gs_ref,
    gp_ref,
    eval_ref,
    p_ref,
    src_b,
    tgt_b,
    q_ref,
    near_ref,
    count_b,
    pat_b,
    gall,
    gf_ref,
    table,
    key_v,
    key_s,
    slot_f,
    msg,
    got,
    rows_ref,
    sums_ref,
    in_sem,
    pos_sem,
    key_sem,
    right_send,
    right_recv,
    left_send,
    left_recv,
    sib_send,
    sib_recv,
    oct_send,
    oct_recv,
):
    o = lax.axis_index("oct")
    c = lax.axis_index("cube")
    boxes, panels = charges_ref.shape
    width = moment_ref.shape[1]
    n_pat = trans_ref.shape[0]
    klist = gs_ref.shape[0]
    fanin = rs_ref.shape[1]
    slots = rs_ref.shape[2]
    chips = n_cube // 2
    right = lax.rem(c + 2, n_cube)
    left = lax.rem(c + n_cube - 2, n_cube)
    sib = c + 1 - 2 * lax.rem(c, 2)

    pairs = (
        (charges_in, charges_ref),
        (counts_in, counts_ref),
        (moment_in, moment_ref),
        (rs_in, rs_ref),
        (rp_in, rp_ref),
        (trans_in, trans_ref),
        (nb_in, nb_ref),
        (rt_in, rt_ref),
        (gs_in, gs_ref),
        (gp_in, gp_ref),
        (eval_in, eval_ref),
    )
    copies = [pltpu.make_async_copy(a, b, in_sem.at[i]) for i, (a, b) in enumerate(pairs)]
    pos_copies = [
        pltpu.make_async_copy(pos_ref.at[d], p_ref.at[:, d + 4 * e], pos_sem.at[d + 3 * e])
        for d in range(3)
        for e in range(2)
    ]
    for copy in copies[:5] + pos_copies + copies[5:]:
        copy.start()

    barrier = pltpu.get_barrier_semaphore()
    for peer in (right, left, sib):
        pl.semaphore_signal(barrier, inc=1, device_id={"cube": peer}, device_id_type=MESH)
    for i in range(n_oct - 1):
        d = lax.rem(o + 1 + i, n_oct)
        pl.semaphore_signal(barrier, inc=1, device_id={"oct": d}, device_id_type=MESH)

    lane = lax.broadcasted_iota(I32, (8, 128), 1)
    sub = lax.broadcasted_iota(I32, (8, 128), 0)

    for copy in copies[:5]:
        copy.wait()
    key_v[...] = rp_ref[...] * boxes + rs_ref[...]
    key_copy = pltpu.make_async_copy(key_v, key_s, key_sem.at[0])
    key_copy.start()
    lane_big = lax.broadcasted_iota(I32, (128, 128), 1)
    for h in range(boxes // 128):
        half = slice(128 * h, 128 * h + 128)
        count_b[half] = column(counts_ref[h : h + 1, :])
        charge = charges_ref[half].astype(F32)
        q_ref[half] = jnp.where(lane_big < count_b[half], charge, 0.0)
    strength = q_ref[...].astype(BF16)
    multipole = jnp.dot(strength, moment_ref[...], preferred_element_type=F32).astype(BF16)
    gall[c] = multipole
    for copy in copies[5:]:
        copy.wait()
    for p in range(n_pat):
        table[p * boxes : (p + 1) * boxes] = jnp.dot(
            multipole, trans_ref[p], preferred_element_type=F32
        )
    for copy in pos_copies:
        copy.wait()

    targets = rt_ref[...].astype(F32)
    blank = jnp.zeros_like(targets)
    odd = lax.rem(o, 2)
    target_rows = jnp.where(
        odd == 0,
        jnp.concatenate([targets, blank], axis=1),
        jnp.concatenate([blank, targets], axis=1),
    )
    for d in range(n_oct):
        msg[d, slots : slots + 16, :] = jnp.broadcast_to(
            target_rows[d : d + 1], (16, 2 * slots)
        ).astype(BF16)
    key_copy.wait()
    groups_each = boxes // (4 * n_oct)

    def one_group(d, carry):
        for j in range(slots):
            total = None
            for k in range(fanin):
                row = table[pl.ds(key_s[d, k, j], 1), :]
                total = row if total is None else total + row
            slot_f[j : j + 1, :] = total
        for u in range(groups_each):
            features_of_four(d * groups_each + u, p_ref, src_b, tgt_b, sub)
        msg[d, 0:slots, :] = slot_f[...].astype(BF16)
        return carry

    lax.fori_loop(0, n_oct, one_group, 0)
    for k in range(klist):
        for h in range(boxes // 128):
            pat_b[k, 128 * h : 128 * h + 128] = column(gp_ref[k : k + 1, 128 * h : 128 * h + 128])

    pl.semaphore_wait(barrier, 3 + n_oct - 1)

    def send(shard, peer, sends, recvs, n):
        return pltpu.make_async_remote_copy(
            src_ref=gall.at[shard],
            dst_ref=gall.at[shard],
            send_sem=sends.at[n],
            recv_sem=recvs.at[n],
            device_id={"cube": peer},
            device_id_type=MESH,
        )

    n_right = chips // 2
    n_left = chips - 1 - n_right
    from_left = [lax.rem(c + n_cube - 2 * h, n_cube) for h in range(n_right + 1)]
    from_right = [lax.rem(c + 2 * h, n_cube) for h in range(n_left + 1)]
    to_right = [send(from_left[h], right, right_send, right_recv, h) for h in range(n_right)]
    to_left = [send(from_right[h], left, left_send, left_recv, h) for h in range(n_left)]
    to_sib = [send(from_left[h], sib, sib_send, sib_recv, h) for h in range(n_right + 1)]
    to_sib += [
        send(from_right[h], sib, sib_send, sib_recv, n_right + h) for h in range(1, n_left + 1)
    ]

    to_right[0].start()
    to_left[0].start()
    to_sib[0].start()

    def ring_step(h):
        if h <= n_right:
            to_right[h - 1].wait_recv()
        if h <= n_left:
            to_left[h - 1].wait_recv()
        if h < n_right:
            to_right[h].start()
        if h < n_left:
            to_left[h].start()
        if h <= n_right:
            to_sib[h].start()
        if h <= n_left:
            to_sib[n_right + h].start()

    def to_oct(i):
        d = lax.rem(o + 1 + i, n_oct)
        return pltpu.make_async_remote_copy(
            src_ref=msg.at[d],
            dst_ref=got.at[o],
            send_sem=oct_send.at[i],
            recv_sem=oct_recv.at[i],
            device_id={"oct": d},
            device_id_type=MESH,
        )

    for i in range(n_oct - 1):
        to_oct(i).start()
    got[o] = msg[o]

    def near_step(i, carry):
        for h in range(1, n_right + 1):

            @pl.when(i == h + RING_FROM)
            def _(h=h):
                ring_step(h)

        near_boxes_step(i, nb_ref, q_ref, src_b, tgt_b, near_ref, lane, sub)
        return carry

    lax.fori_loop(0, boxes // NEAR_UNROLL, near_step, 0)

    for copy in to_sib:
        copy.wait_recv()
    gf_ref[...] = gall[...].reshape(n_cube * boxes, width).astype(F32)

    def gather(i, carry):
        t0 = pl.multiple_of(16 * i, 16)
        for u in range(16):
            for k in range(klist):
                rows_ref[k, pl.ds(t0 + u, 1), :] = gf_ref[pl.ds(gs_ref[k, t0 + u], 1), :]
        return carry

    lax.fori_loop(0, boxes // 16, gather, 0)

    def pattern_sums(i, carry):
        t0 = pl.ds(pl.multiple_of(16 * i, 16), 16)
        pats = [pat_b[k, t0] for k in range(klist)]
        rows = [rows_ref[k, t0] for k in range(klist)]
        for p in range(n_pat):
            total = None
            for k in range(klist):
                x = jnp.where(pats[k] == p, rows[k], 0.0)
                total = x if total is None else total + x
            sums_ref[t0, p * width : (p + 1) * width] = total.astype(BF16)
        return carry

    lax.fori_loop(0, boxes // 16, pattern_sums, 0)
    operators = trans_ref[...].reshape(n_pat * width, width)
    local = jnp.dot(sums_ref[...], operators, preferred_element_type=F32)

    for i in range(n_oct - 1):
        to_oct(i).wait_recv()
    box = lax.broadcasted_iota(I32, (boxes, 2 * slots), 0).astype(F32)
    for m in range(n_oct // 4):
        hot, vals = [], []
        for e in (4 * m, 4 * m + 2):
            trow = got[e, slots : slots + 16, :].astype(F32) + got[
                e + 1, slots : slots + 16, :
            ].astype(F32)
            hot.append(jnp.where(box == trow[0:1], 1.0, 0.0).astype(BF16))
            vals += [got[e, 0:slots, :], got[e + 1, 0:slots, :]]
        local = local + jnp.dot(
            jnp.concatenate(hot, axis=1),
            jnp.concatenate(vals, axis=0),
            preferred_element_type=F32,
        )

    far = jnp.dot(local.astype(BF16), eval_ref[...], preferred_element_type=F32)
    total = near_ref[...] * (1.0 / (4.0 * math.pi)) + far
    panel = lax.broadcasted_iota(I32, (boxes, panels), 1)
    out_ref[...] = jnp.where(panel < count_b[...], total, 0.0)

    for copy in to_right + to_left + to_sib:
        copy.wait_send()
    for i in range(n_oct - 1):
        to_oct(i).wait_send()


def body(
    n_oct,
    n_cube,
    charges,
    panel_counts,
    positions,
    moment_map,
    translations,
    evaluation,
    near_boxes,
    group_sources,
    group_patterns,
    remote_sources,
    remote_patterns,
    remote_targets,
):
    boxes, panels = charges.shape
    width = moment_map.shape[1]
    n_pat = translations.shape[0]
    klist = group_sources.shape[1]
    slots, fanin = remote_sources.shape[3:]
    chips = n_cube // 2
    sources = remote_sources[0, 0].transpose(0, 2, 1)
    patterns = remote_patterns[0, 0].transpose(0, 2, 1)
    dma = pltpu.SemaphoreType.DMA
    return pl.pallas_call(
        functools.partial(step_kernel, n_oct, n_cube),
        out_shape=jax.ShapeDtypeStruct((boxes, panels), F32),
        in_specs=[pl.BlockSpec(memory_space=pltpu.HBM)] * 12,
        out_specs=pl.BlockSpec(memory_space=pltpu.VMEM),
        scratch_shapes=[
            pltpu.VMEM((boxes, panels), BF16),
            pltpu.VMEM((boxes // 128, 128), I32),
            pltpu.VMEM((panels, width), BF16),
            pltpu.VMEM((n_pat, width, width), BF16),
            pltpu.VMEM((n_oct, fanin, slots), I32),
            pltpu.VMEM((n_oct, fanin, slots), I32),
            pltpu.SMEM((near_boxes.shape[1], boxes), I32),
            pltpu.VMEM((n_oct, slots), I32),
            pltpu.SMEM((klist, boxes), I32),
            pltpu.VMEM((klist, boxes), I32),
            pltpu.VMEM((width, panels), BF16),
            pltpu.VMEM((boxes, 8, panels), F32),
            pltpu.VMEM((boxes, FEAT, panels), BF16),
            pltpu.VMEM((boxes // 4, panels, 4 * FEAT), BF16),
            pltpu.VMEM((boxes, panels), F32),
            pltpu.VMEM((boxes, panels), F32),
            pltpu.VMEM((boxes, panels), I32),
            pltpu.VMEM((klist, boxes, width), I32),
            pltpu.VMEM((n_cube, boxes, width), BF16),
            pltpu.VMEM((n_cube * boxes, width), F32),
            pltpu.VMEM((n_pat * boxes, width), F32),
            pltpu.VMEM((n_oct, fanin, slots), I32),
            pltpu.SMEM((n_oct, fanin, slots), I32),
            pltpu.VMEM((slots, width), F32),
            pltpu.VMEM((n_oct, slots + 16, width), BF16),
            pltpu.VMEM((n_oct, slots + 16, width), BF16),
            pltpu.VMEM((klist, boxes, width), F32),
            pltpu.VMEM((boxes, n_pat * width), BF16),
            dma((11,)),
            dma((6,)),
            dma((1,)),
            dma((chips,)),
            dma((chips,)),
            dma((chips,)),
            dma((chips,)),
            dma((chips,)),
            dma((chips,)),
            dma((n_oct,)),
            dma((n_oct,)),
        ],
        compiler_params=pltpu.CompilerParams(
            collective_id=0, has_side_effects=True, vmem_limit_bytes=62 << 20
        ),
    )(
        positions,
        charges,
        panel_counts.reshape(boxes // 128, 128),
        moment_map,
        translations,
        sources,
        patterns,
        near_boxes.T,
        remote_targets[0, 0],
        group_sources.T,
        group_patterns.T,
        evaluation,
    )


def solution(mesh):
    n_oct, n_cube = mesh.shape["oct"], mesh.shape["cube"]
    return jax.shard_map(
        functools.partial(body, n_oct, n_cube),
        mesh=mesh,
        in_specs=(
            P(("oct", "cube"), None),
            P(("oct", "cube")),
            P(None, ("oct", "cube"), None),
            P(),
            P(),
            P(),
            P(("oct", "cube"), None),
            P(("oct", "cube"), None),
            P(("oct", "cube"), None),
            P("oct", "cube", None, None, None),
            P("oct", "cube", None, None, None),
            P("oct", "cube", None, None),
        ),
        out_specs=P(("oct", "cube"), None),
        check_vma=False,
    )
```

```python
import functools
import math

import jax
import jax.numpy as jnp
from jax import lax
from jax.experimental import pallas as pl
from jax.experimental.pallas import tpu as pltpu
from jax.sharding import PartitionSpec as P

F32, BF16, I32 = jnp.float32, jnp.bfloat16, jnp.int32
MESH = pl.DeviceIdType.MESH
FEAT = 32
SOFT = 0.0025
NEAR_UNROLL = 32
CHIP_SENDS = ((0, 1), (0, -1), (0, 2), (0, -2), (-2, 1), (-2, 2), (2, -1))
PASS_ON = (((6, 6), (2, 3, 0, 1)), ((7, 0), (4, 5, 6)))


def parts3(v):
    hi = v.astype(BF16).astype(F32)
    rest = v - hi
    mid = rest.astype(BF16).astype(F32)
    return hi, mid, rest - mid


def merge(a, b, first, shift, axis):
    return jnp.where(first, a, b) + pltpu.roll(jnp.where(first, b, a), shift, axis)


def column(row):
    return jnp.broadcast_to(row, (128, 128)).T


def features_of_four(i, p_ref, src_b, tgt_b, sub):
    is3, is7, lo3, lo4 = sub == 3, sub == 7, sub < 3, sub < 4
    pad = is3 | is7
    zero = jnp.zeros((8, 128), F32)
    cols = []
    for u in range(4):
        t = 4 * i + u
        v = jnp.where(pad, 0.0, p_ref[t] - 1.0)
        s = v * v
        s = s + pltpu.roll(s, 1, 0)
        n = s + pltpu.roll(s, 2, 0)
        w1, w2, w3 = parts3(jnp.where(pad, n, v))
        s0 = jnp.where(is7, 1.0, w1)
        s1 = jnp.where(is7, 1.0, w2)
        s2 = jnp.where(is7, 1.0, jnp.where(lo3, w1, w3))
        src_b[t] = jnp.concatenate([s0, s1, s2, zero], axis=0).astype(BF16)
        m1, m2, m3 = parts3(n + SOFT)
        y1, y2, y3 = -2.0 * w1, -2.0 * w2, -2.0 * w3
        base = jnp.where(is3, 1.0, jnp.where(lo4, y1, y2))
        t0 = jnp.where(is7, m1, base)
        t1 = jnp.where(is7, m2, base)
        t2 = jnp.where(is7, m3, jnp.where(is3, 1.0, jnp.where(lo4, y3, y1)))
        cols += [t0, t1, t2, zero]
    tgt_b[i] = jnp.concatenate(cols, axis=0).T.astype(BF16)


def near_boxes_step(i, nb_ref, q_ref, src_b, tgt_b, near_ref, lane, sub):
    t0 = pl.multiple_of(NEAR_UNROLL * i, NEAR_UNROLL)
    knear = nb_ref.shape[0]
    rows = []
    for u in range(NEAR_UNROLL):
        lhs = tgt_b[(NEAR_UNROLL // 4) * i + u // 4]
        lo = FEAT * (u % 4)
        acc = None
        for pair in range(knear // 2):
            ids = [nb_ref[2 * pair + e, t0 + u] for e in range(2)]
            parts = [jnp.concatenate([src_b[s] for s in ids], axis=1)]
            if lo:
                parts.insert(0, jnp.zeros((lo, 256), BF16))
            if lo + FEAT < 128:
                parts.append(jnp.zeros((128 - FEAT - lo, 256), BF16))
            rhs = jnp.concatenate(parts, axis=0)
            inv = lax.rsqrt(jnp.dot(lhs, rhs, preferred_element_type=F32))
            for e in range(2):
                q = q_ref[pl.ds(ids[e], 1), :]
                term = inv[:, 128 * e : 128 * e + 128] * q
                acc = term if acc is None else acc + term
        row = None
        for g in range(16):
            total = jnp.sum(acc[8 * g : 8 * g + 8], axis=1, keepdims=True)
            x = jnp.where(lane == sub + 8 * g, total, 0.0)
            row = x if row is None else row + x
        rows.append(row)
    for b in range(NEAR_UNROLL // 8):
        some = rows[8 * b : 8 * b + 8]
        shift = 1
        while len(some) > 1:
            first = (sub & shift) == 0
            some = [merge(some[2 * n], some[2 * n + 1], first, shift, 0) for n in range(len(some) // 2)]
            shift *= 2
        near_ref[pl.ds(t0 + 8 * b, 8), :] = some[0]


def step_kernel(
    n_oct,
    n_cube,
    pos_ref,
    charges_in,
    counts_in,
    moment_in,
    trans_in,
    rs_in,
    rp_in,
    nb_in,
    rt_in,
    gs_in,
    gp_in,
    eval_in,
    out_ref,
    charges_ref,
    counts_ref,
    moment_ref,
    trans_ref,
    rs_ref,
    rp_ref,
    nb_ref,
    rt_ref,
    gs_ref,
    gp_ref,
    eval_ref,
    p_ref,
    src_b,
    tgt_b,
    q_ref,
    near_ref,
    count_b,
    pat_b,
    gall,
    gf_ref,
    table,
    key_v,
    key_s,
    slot_f,
    msg,
    got,
    rows_ref,
    sums_ref,
    remote_ref,
    in_sem,
    pos_sem,
    key_sem,
    chip_send,
    chip_recv,
    sib_send,
    sib_recv,
    oct_send,
    oct_recv,
):
    o = lax.axis_index("oct")
    c = lax.axis_index("cube")
    boxes, panels = charges_ref.shape
    width = moment_ref.shape[1]
    n_pat = trans_ref.shape[0]
    klist = gs_ref.shape[0]
    fanin = rs_ref.shape[1]
    slots = rs_ref.shape[2]
    sib = c + 1 - 2 * lax.rem(c, 2)

    pairs = (
        (charges_in, charges_ref),
        (counts_in, counts_ref),
        (moment_in, moment_ref),
        (rs_in, rs_ref),
        (rp_in, rp_ref),
        (trans_in, trans_ref),
        (nb_in, nb_ref),
        (rt_in, rt_ref),
        (gs_in, gs_ref),
        (gp_in, gp_ref),
        (eval_in, eval_ref),
    )
    copies = [pltpu.make_async_copy(a, b, in_sem.at[i]) for i, (a, b) in enumerate(pairs)]
    pos_copies = [
        pltpu.make_async_copy(pos_ref.at[d], p_ref.at[:, d + 4 * e], pos_sem.at[d + 3 * e])
        for d in range(3)
        for e in range(2)
    ]
    for copy in copies[:5] + pos_copies + copies[5:]:
        copy.start()

    barrier = pltpu.get_barrier_semaphore()
    dests = sorted({d % (n_cube // 2) for _, d in CHIP_SENDS} | {-d % (n_cube // 2) for _, d in CHIP_SENDS})
    for peer in [sib] + [lax.rem(c + 2 * d, n_cube) for d in dests]:
        pl.semaphore_signal(barrier, inc=1, device_id={"cube": peer}, device_id_type=MESH)
    for i in range(n_oct - 1):
        d = lax.rem(o + 1 + i, n_oct)
        pl.semaphore_signal(barrier, inc=1, device_id={"oct": d}, device_id_type=MESH)

    lane = lax.broadcasted_iota(I32, (8, 128), 1)
    sub = lax.broadcasted_iota(I32, (8, 128), 0)

    for copy in copies[:5]:
        copy.wait()
    key_v[...] = rp_ref[...] * boxes + rs_ref[...]
    key_copy = pltpu.make_async_copy(key_v, key_s, key_sem.at[0])
    key_copy.start()
    lane_big = lax.broadcasted_iota(I32, (128, 128), 1)
    for h in range(boxes // 128):
        half = slice(128 * h, 128 * h + 128)
        count_b[half] = column(counts_ref[h : h + 1, :])
        charge = charges_ref[half].astype(F32)
        q_ref[half] = jnp.where(lane_big < count_b[half], charge, 0.0)
    strength = q_ref[...].astype(BF16)
    multipole = jnp.dot(strength, moment_ref[...], preferred_element_type=F32).astype(BF16)
    gall[c] = multipole
    for copy in copies[5:]:
        copy.wait()
    for p in range(n_pat):
        table[p * boxes : (p + 1) * boxes] = jnp.dot(
            multipole, trans_ref[p], preferred_element_type=F32
        )
    for copy in pos_copies:
        copy.wait()

    targets = rt_ref[...].astype(F32)
    blank = jnp.zeros_like(targets)
    odd = lax.rem(o, 2)
    target_rows = jnp.where(
        odd == 0,
        jnp.concatenate([targets, blank], axis=1),
        jnp.concatenate([blank, targets], axis=1),
    )
    for d in range(n_oct):
        msg[d, slots : slots + 16, :] = jnp.broadcast_to(
            target_rows[d : d + 1], (16, 2 * slots)
        ).astype(BF16)
    key_copy.wait()
    groups_each = boxes // (4 * n_oct)

    def one_group(d, carry):
        for j in range(slots):
            total = None
            for k in range(fanin):
                row = table[pl.ds(key_s[d, k, j], 1), :]
                total = row if total is None else total + row
            slot_f[j : j + 1, :] = total
        for u in range(groups_each):
            features_of_four(d * groups_each + u, p_ref, src_b, tgt_b, sub)
        msg[d, 0:slots, :] = slot_f[...].astype(BF16)
        return carry

    lax.fori_loop(0, n_oct, one_group, 0)
    for k in range(klist):
        for h in range(boxes // 128):
            pat_b[k, 128 * h : 128 * h + 128] = column(gp_ref[k : k + 1, 128 * h : 128 * h + 128])

    def shard_at(off):
        return lax.rem(c + 2 * off + n_cube, n_cube)

    def send(off, peer, sends, recvs, n):
        shard = shard_at(off)
        return pltpu.make_async_remote_copy(
            src_ref=gall.at[shard],
            dst_ref=gall.at[shard],
            send_sem=sends.at[n],
            recv_sem=recvs.at[n],
            device_id={"cube": peer},
            device_id_type=MESH,
        )

    to_chip = [send(s, shard_at(d), chip_send, chip_recv, n) for n, (s, d) in enumerate(CHIP_SENDS)]
    brought = [s - d for s, d in CHIP_SENDS]
    to_sib = [send(s, sib, sib_send, sib_recv, n) for n, s in enumerate(brought + [0])]

    def widen(off, other):
        shard = shard_at(off)
        if other:
            shard = shard + 1 - 2 * lax.rem(c, 2)
        rows = pl.ds(pl.multiple_of(shard * boxes, boxes), boxes)
        gf_ref[rows, :] = gall[shard].astype(F32)

    def pass_on(arrived):
        for n in arrived:
            to_chip[n].wait_recv()
            for m, (s, d) in enumerate(CHIP_SENDS):
                if s != 0 and s == brought[n]:
                    to_chip[m].start()
            to_sib[n].start()
            widen(brought[n], False)

    def to_oct(i):
        d = lax.rem(o + 1 + i, n_oct)
        return pltpu.make_async_remote_copy(
            src_ref=msg.at[d],
            dst_ref=got.at[o],
            send_sem=oct_send.at[i],
            recv_sem=oct_recv.at[i],
            device_id={"oct": d},
            device_id_type=MESH,
        )

    got[o] = msg[o]

    def open_up():
        pl.semaphore_wait(barrier, 1 + len(dests) + n_oct - 1)
        for n, (s, d) in enumerate(CHIP_SENDS):
            if s == 0:
                to_chip[n].start()
        to_sib[-1].start()
        for i in range(n_oct - 1):
            to_oct(i).start()

    open_up()

    def near_step(i, carry):
        for when, arrived in PASS_ON:

            @pl.when(i == when[0] - (c // 2) * when[1] // (n_cube // 2))
            def _(arrived=arrived):
                pass_on(arrived)

        near_boxes_step(i, nb_ref, q_ref, src_b, tgt_b, near_ref, lane, sub)
        return carry

    lax.fori_loop(0, boxes // NEAR_UNROLL, near_step, 0)

    for i in range(n_oct - 1):
        to_oct(i).wait_recv()
    box = lax.broadcasted_iota(I32, (boxes, 2 * slots), 0).astype(F32)
    remote = None
    for m in range(n_oct // 4):
        hot, vals = [], []
        for e in (4 * m, 4 * m + 2):
            trow = got[e, slots : slots + 16, :].astype(F32) + got[
                e + 1, slots : slots + 16, :
            ].astype(F32)
            hot.append(jnp.where(box == trow[0:1], 1.0, 0.0).astype(BF16))
            vals += [got[e, 0:slots, :], got[e + 1, 0:slots, :]]
        part = jnp.dot(
            jnp.concatenate(hot, axis=1),
            jnp.concatenate(vals, axis=0),
            preferred_element_type=F32,
        )
        remote = part if remote is None else remote + part
    remote_ref[...] = remote

    widen(0, False)
    for n, off in enumerate(brought + [0]):
        to_sib[n].wait_recv()
        widen(off, True)

    def gather(i, carry):
        t0 = pl.multiple_of(16 * i, 16)
        for u in range(16):
            for k in range(klist):
                rows_ref[k, pl.ds(t0 + u, 1), :] = gf_ref[pl.ds(gs_ref[k, t0 + u], 1), :]
        return carry

    lax.fori_loop(0, boxes // 16, gather, 0)

    def pattern_sums(i, carry):
        t0 = pl.ds(pl.multiple_of(16 * i, 16), 16)
        pats = [pat_b[k, t0] for k in range(klist)]
        rows = [rows_ref[k, t0] for k in range(klist)]
        for p in range(n_pat):
            total = None
            for k in range(klist):
                x = jnp.where(pats[k] == p, rows[k], 0.0)
                total = x if total is None else total + x
            sums_ref[t0, p * width : (p + 1) * width] = total.astype(BF16)
        return carry

    lax.fori_loop(0, boxes // 16, pattern_sums, 0)
    operators = trans_ref[...].reshape(n_pat * width, width)
    local = jnp.dot(sums_ref[...], operators, preferred_element_type=F32) + remote_ref[...]

    far = jnp.dot(local.astype(BF16), eval_ref[...], preferred_element_type=F32)
    total = near_ref[...] * (1.0 / (4.0 * math.pi)) + far
    panel = lax.broadcasted_iota(I32, (boxes, panels), 1)
    out_ref[...] = jnp.where(panel < count_b[...], total, 0.0)

    for copy in to_chip + to_sib:
        copy.wait_send()
    for i in range(n_oct - 1):
        to_oct(i).wait_send()


def body(
    n_oct,
    n_cube,
    charges,
    panel_counts,
    positions,
    moment_map,
    translations,
    evaluation,
    near_boxes,
    group_sources,
    group_patterns,
    remote_sources,
    remote_patterns,
    remote_targets,
):
    boxes, panels = charges.shape
    width = moment_map.shape[1]
    n_pat = translations.shape[0]
    klist = group_sources.shape[1]
    slots, fanin = remote_sources.shape[3:]
    chips = n_cube // 2
    sources = remote_sources[0, 0].transpose(0, 2, 1)
    patterns = remote_patterns[0, 0].transpose(0, 2, 1)
    dma = pltpu.SemaphoreType.DMA
    return pl.pallas_call(
        functools.partial(step_kernel, n_oct, n_cube),
        out_shape=jax.ShapeDtypeStruct((boxes, panels), F32),
        in_specs=[pl.BlockSpec(memory_space=pltpu.HBM)] * 12,
        out_specs=pl.BlockSpec(memory_space=pltpu.VMEM),
        scratch_shapes=[
            pltpu.VMEM((boxes, panels), BF16),
            pltpu.VMEM((boxes // 128, 128), I32),
            pltpu.VMEM((panels, width), BF16),
            pltpu.VMEM((n_pat, width, width), BF16),
            pltpu.VMEM((n_oct, fanin, slots), I32),
            pltpu.VMEM((n_oct, fanin, slots), I32),
            pltpu.SMEM((near_boxes.shape[1], boxes), I32),
            pltpu.VMEM((n_oct, slots), I32),
            pltpu.SMEM((klist, boxes), I32),
            pltpu.VMEM((klist, boxes), I32),
            pltpu.VMEM((width, panels), BF16),
            pltpu.VMEM((boxes, 8, panels), F32),
            pltpu.VMEM((boxes, FEAT, panels), BF16),
            pltpu.VMEM((boxes // 4, panels, 4 * FEAT), BF16),
            pltpu.VMEM((boxes, panels), F32),
            pltpu.VMEM((boxes, panels), F32),
            pltpu.VMEM((boxes, panels), I32),
            pltpu.VMEM((klist, boxes, width), I32),
            pltpu.VMEM((n_cube, boxes, width), BF16),
            pltpu.VMEM((n_cube * boxes, width), F32),
            pltpu.VMEM((n_pat * boxes, width), F32),
            pltpu.VMEM((n_oct, fanin, slots), I32),
            pltpu.SMEM((n_oct, fanin, slots), I32),
            pltpu.VMEM((slots, width), F32),
            pltpu.VMEM((n_oct, slots + 16, width), BF16),
            pltpu.VMEM((n_oct, slots + 16, width), BF16),
            pltpu.VMEM((klist, boxes, width), F32),
            pltpu.VMEM((boxes, n_pat * width), BF16),
            pltpu.VMEM((boxes, width), F32),
            dma((11,)),
            dma((6,)),
            dma((1,)),
            dma((chips,)),
            dma((chips,)),
            dma((chips,)),
            dma((chips,)),
            dma((n_oct,)),
            dma((n_oct,)),
        ],
        compiler_params=pltpu.CompilerParams(
            collective_id=0, has_side_effects=True, vmem_limit_bytes=62 << 20
        ),
    )(
        positions,
        charges,
        panel_counts.reshape(boxes // 128, 128),
        moment_map,
        translations,
        sources,
        patterns,
        near_boxes.T,
        remote_targets[0, 0],
        group_sources.T,
        group_patterns.T,
        evaluation,
    )


def solution(mesh):
    n_oct, n_cube = mesh.shape["oct"], mesh.shape["cube"]
    return jax.shard_map(
        functools.partial(body, n_oct, n_cube),
        mesh=mesh,
        in_specs=(
            P(("oct", "cube"), None),
            P(("oct", "cube")),
            P(None, ("oct", "cube"), None),
            P(),
            P(),
            P(),
            P(("oct", "cube"), None),
            P(("oct", "cube"), None),
            P(("oct", "cube"), None),
            P("oct", "cube", None, None, None),
            P("oct", "cube", None, None, None),
            P("oct", "cube", None, None),
        ),
        out_specs=P(("oct", "cube"), None),
        check_vma=False,
    )
```

```python
import functools
import math

import jax
import jax.numpy as jnp
from jax import lax
from jax.experimental import pallas as pl
from jax.experimental.pallas import tpu as pltpu
from jax.sharding import PartitionSpec as P

F32, BF16, I32 = jnp.float32, jnp.bfloat16, jnp.int32
MESH = pl.DeviceIdType.MESH
FEAT = 32
SOFT = 0.0025
BLOCK = 32
CHIP_SENDS = ((0, 1), (0, -1), (0, 2), (0, -2), (-2, 1), (-2, 2), (2, -1))
PASS_ON = (((5, 5), (2, 3, 0, 1)), ((7, 2), (4, 5, 6)))


def parts3(v):
    hi = v.astype(BF16).astype(F32)
    rest = v - hi
    mid = rest.astype(BF16).astype(F32)
    return hi, mid, rest - mid


def merge(a, b, first, shift, axis):
    return jnp.where(first, a, b) + pltpu.roll(jnp.where(first, b, a), shift, axis)


def halves(word):
    return word & 65535, lax.shift_right_logical(word, 16)


def column(row):
    return jnp.broadcast_to(row, (128, 128)).T


def features_of_four(i, p_ref, src_b, tgt_b, sub):
    is3, is7, lo3, lo4 = sub == 3, sub == 7, sub < 3, sub < 4
    pad = is3 | is7
    zero = jnp.zeros((8, 128), F32)
    cols = []
    for u in range(4):
        t = 4 * i + u
        v = jnp.where(pad, 0.0, p_ref[t] - 1.0)
        s = v * v
        s = s + pltpu.roll(s, 1, 0)
        n = s + pltpu.roll(s, 2, 0)
        w1, w2, w3 = parts3(jnp.where(pad, n, v))
        s0 = jnp.where(is7, 1.0, w1)
        s1 = jnp.where(is7, 1.0, w2)
        s2 = jnp.where(is7, 1.0, jnp.where(lo3, w1, w3))
        src_b[t] = jnp.concatenate([s0, s1, s2, zero], axis=0).astype(BF16)
        m1, m2, m3 = parts3(n + SOFT)
        y1, y2, y3 = -2.0 * w1, -2.0 * w2, -2.0 * w3
        base = jnp.where(is3, 1.0, jnp.where(lo4, y1, y2))
        t0 = jnp.where(is7, m1, base)
        t1 = jnp.where(is7, m2, base)
        t2 = jnp.where(is7, m3, jnp.where(is3, 1.0, jnp.where(lo4, y3, y1)))
        cols += [t0, t1, t2, zero]
    tgt_b[i] = jnp.concatenate(cols, axis=0).T.astype(BF16)


def near_boxes_step(i, nb_ref, q_ref, src_b, tgt_b, near_ref, lane, sub):
    t0 = pl.multiple_of(BLOCK * i, BLOCK)
    rows = []
    for u in range(BLOCK):
        lhs = tgt_b[(BLOCK // 4) * i + u // 4]
        lo = FEAT * (u % 4)
        acc = None
        word = nb_ref[i, 0, u]
        for pair in range(2):
            ids = [lax.shift_right_logical(word, 16 * pair + 8 * e) & 255 for e in range(2)]
            parts = [jnp.concatenate([src_b[s] for s in ids], axis=1)]
            if lo:
                parts.insert(0, jnp.zeros((lo, 256), BF16))
            if lo + FEAT < 128:
                parts.append(jnp.zeros((128 - FEAT - lo, 256), BF16))
            rhs = jnp.concatenate(parts, axis=0)
            inv = lax.rsqrt(jnp.dot(lhs, rhs, preferred_element_type=F32))
            for e in range(2):
                q = q_ref[pl.ds(ids[e], 1), :]
                term = inv[:, 128 * e : 128 * e + 128] * q
                acc = term if acc is None else acc + term
        row = None
        for g in range(16):
            total = jnp.sum(acc[8 * g : 8 * g + 8], axis=1, keepdims=True)
            x = jnp.where(lane == sub + 8 * g, total, 0.0)
            row = x if row is None else row + x
        rows.append(row)
    for b in range(BLOCK // 8):
        some = rows[8 * b : 8 * b + 8]
        shift = 1
        while len(some) > 1:
            first = (sub & shift) == 0
            some = [merge(some[2 * n], some[2 * n + 1], first, shift, 0) for n in range(len(some) // 2)]
            shift *= 2
        near_ref[pl.ds(t0 + 8 * b, 8), :] = some[0]


def step_kernel(
    n_oct,
    n_cube,
    pos_ref,
    charges_in,
    counts_in,
    moment_in,
    trans_in,
    rs_in,
    rp_in,
    nb_in,
    rt_in,
    gs_in,
    gp_in,
    eval_in,
    out_ref,
    charges_ref,
    counts_ref,
    moment_ref,
    trans_ref,
    rs_ref,
    rp_ref,
    nb_ref,
    rt_ref,
    gs_ref,
    gp_ref,
    eval_ref,
    nb_v,
    nb_s,
    gs_v,
    gs_s,
    p_ref,
    src_b,
    tgt_b,
    q_ref,
    near_ref,
    count_b,
    gall,
    gf_ref,
    table,
    key_v,
    key_s,
    slot_f,
    msg,
    got,
    rows_a,
    rows_b,
    hot_ref,
    sums_ref,
    remote_ref,
    in_sem,
    pos_sem,
    key_sem,
    chip_send,
    chip_recv,
    sib_send,
    sib_recv,
    oct_send,
    oct_recv,
):
    o = lax.axis_index("oct")
    c = lax.axis_index("cube")
    boxes, panels = charges_ref.shape
    width = moment_ref.shape[1]
    n_pat = trans_ref.shape[0]
    klist = gs_ref.shape[0]
    fanin = rs_ref.shape[1]
    slots = rs_ref.shape[2]
    sib = c + 1 - 2 * lax.rem(c, 2)

    pairs = (
        (charges_in, charges_ref),
        (counts_in, counts_ref),
        (moment_in, moment_ref),
        (rs_in, rs_ref),
        (rp_in, rp_ref),
        (trans_in, trans_ref),
        (nb_in, nb_ref),
        (rt_in, rt_ref),
        (gs_in, gs_ref),
        (gp_in, gp_ref),
        (eval_in, eval_ref),
    )
    copies = [pltpu.make_async_copy(a, b, in_sem.at[i]) for i, (a, b) in enumerate(pairs)]
    pos_copies = [
        pltpu.make_async_copy(pos_ref.at[d], p_ref.at[:, d + 4 * e], pos_sem.at[d + 3 * e])
        for d in range(3)
        for e in range(2)
    ]
    for copy in copies[:5] + pos_copies + copies[5:]:
        copy.start()

    barrier = pltpu.get_barrier_semaphore()
    dests = sorted({d % (n_cube // 2) for _, d in CHIP_SENDS} | {-d % (n_cube // 2) for _, d in CHIP_SENDS})
    for peer in [sib] + [lax.rem(c + 2 * d, n_cube) for d in dests]:
        pl.semaphore_signal(barrier, inc=1, device_id={"cube": peer}, device_id_type=MESH)
    for i in range(n_oct - 1):
        d = lax.rem(o + 1 + i, n_oct)
        pl.semaphore_signal(barrier, inc=1, device_id={"oct": d}, device_id_type=MESH)

    lane = lax.broadcasted_iota(I32, (8, 128), 1)
    sub = lax.broadcasted_iota(I32, (8, 128), 0)

    for copy in copies[:5]:
        copy.wait()
    key = rp_ref[...] * boxes + rs_ref[...]
    key_v[...] = key[:, : fanin // 2] + key[:, fanin // 2 :] * 65536
    key_copy = pltpu.make_async_copy(key_v, key_s, key_sem.at[0])
    key_copy.start()
    lane_big = lax.broadcasted_iota(I32, (128, 128), 1)
    for h in range(boxes // 128):
        half = slice(128 * h, 128 * h + 128)
        count_b[half] = column(counts_ref[h : h + 1, :])
        charge = charges_ref[half].astype(F32)
        q_ref[half] = jnp.where(lane_big < count_b[half], charge, 0.0)
    strength = q_ref[...].astype(BF16)
    multipole = jnp.dot(strength, moment_ref[...], preferred_element_type=F32).astype(BF16)
    gall[c] = multipole
    for copy in copies[5:]:
        copy.wait()
    index_copies = []
    def four_bytes(v):
        return v[0:1] + v[1:2] * 256 + v[2:3] * 65536 + v[3:4] * 16777216

    def two_halves(v):
        return v[: klist // 2] + v[klist // 2 :] * 65536

    lists = ((nb_ref, nb_v, nb_s, four_bytes), (gs_ref, gs_v, gs_s, two_halves))
    for n, (whole, cut, scalar, packed) in enumerate(lists):
        for h in range(boxes // 128):
            entries = whole[:, 128 * h : 128 * h + 128]
            for e in range(128 // BLOCK):
                turn = (128 - BLOCK * e) % 128
                mine = pltpu.roll(entries, turn, 1) if turn else entries
                cut[h * (128 // BLOCK) + e] = packed(mine)
        index_copies.append(pltpu.make_async_copy(cut, scalar, key_sem.at[1 + n]))
        index_copies[-1].start()
    for p in range(n_pat):
        table[p * boxes : (p + 1) * boxes] = jnp.dot(
            multipole, trans_ref[p], preferred_element_type=F32
        )
    for copy in pos_copies:
        copy.wait()

    targets = rt_ref[...].astype(F32)
    blank = jnp.zeros_like(targets)
    odd = lax.rem(o, 2)
    target_rows = jnp.where(
        odd == 0,
        jnp.concatenate([targets, blank], axis=1),
        jnp.concatenate([blank, targets], axis=1),
    )
    for d in range(n_oct):
        msg[d, slots : slots + 16, :] = jnp.broadcast_to(
            target_rows[d : d + 1], (16, 2 * slots)
        ).astype(BF16)
    key_copy.wait()
    for copy in index_copies:
        copy.wait()
    groups_each = boxes // (4 * n_oct)

    def one_group(d, carry):
        for j in range(slots):
            total = None
            for k in range(fanin // 2):
                for at in halves(key_s[d, k, j]):
                    row = table[pl.ds(at, 1), :]
                    total = row if total is None else total + row
            slot_f[j : j + 1, :] = total
        for u in range(groups_each):
            features_of_four(d * groups_each + u, p_ref, src_b, tgt_b, sub)
        msg[d, 0:slots, :] = slot_f[...].astype(BF16)
        return carry

    lax.fori_loop(0, n_oct, one_group, 0)
    def shard_at(off):
        return lax.rem(c + 2 * off + n_cube, n_cube)

    def send(off, peer, sends, recvs, n):
        shard = shard_at(off)
        return pltpu.make_async_remote_copy(
            src_ref=gall.at[shard],
            dst_ref=gall.at[shard],
            send_sem=sends.at[n],
            recv_sem=recvs.at[n],
            device_id={"cube": peer},
            device_id_type=MESH,
        )

    to_chip = [send(s, shard_at(d), chip_send, chip_recv, n) for n, (s, d) in enumerate(CHIP_SENDS)]
    brought = [s - d for s, d in CHIP_SENDS]
    to_sib = [send(s, sib, sib_send, sib_recv, n) for n, s in enumerate(brought + [0])]

    def widen(off, other):
        shard = shard_at(off)
        if other:
            shard = shard + 1 - 2 * lax.rem(c, 2)
        rows = pl.ds(pl.multiple_of(shard * boxes, boxes), boxes)
        gf_ref[rows, :] = gall[shard].astype(F32)

    def pass_on(arrived):
        for n in arrived:
            to_chip[n].wait_recv()
            for m, (s, d) in enumerate(CHIP_SENDS):
                if s != 0 and s == brought[n]:
                    to_chip[m].start()
            to_sib[n].start()
            widen(brought[n], False)

    def to_oct(i):
        d = lax.rem(o + 1 + i, n_oct)
        return pltpu.make_async_remote_copy(
            src_ref=msg.at[d],
            dst_ref=got.at[o],
            send_sem=oct_send.at[i],
            recv_sem=oct_recv.at[i],
            device_id={"oct": d},
            device_id_type=MESH,
        )

    got[o] = msg[o]

    def open_up():
        pl.semaphore_wait(barrier, 1 + len(dests) + n_oct - 1)
        for n, (s, d) in enumerate(CHIP_SENDS):
            if s == 0:
                to_chip[n].start()
        to_sib[-1].start()
        for i in range(n_oct - 1):
            to_oct(i).start()

    open_up()

    lane_row = lax.broadcasted_iota(I32, (1, 128), 1)
    lane_blk = lax.broadcasted_iota(I32, (BLOCK, 128), 1)
    own = lax.rem(lane_blk, BLOCK) == lax.broadcasted_iota(I32, (BLOCK, 128), 0)
    per = 128 // BLOCK
    for h in range(boxes // 128):
        entries = gp_ref[:, 128 * h : 128 * h + 128]
        turned = [entries] + [pltpu.roll(entries, BLOCK * s, 1) for s in range(1, per)]
        for e in range(per):
            for half in range(klist // per):
                row = None
                for j in range(per):
                    piece = turned[(j - e) % per][per * half + j : per * half + j + 1]
                    row = piece if row is None else jnp.where(lane_row // BLOCK == j, piece, row)
                wanted = jnp.where(own, row, -1)
                for p in range(n_pat):
                    hot_ref[per * h + e, BLOCK * p : BLOCK * (p + 1), 128 * half : 128 * half + 128] = (
                        jnp.where(wanted == p, 1.0, 0.0).astype(BF16)
                    )

    def near_step(i, carry):
        for when, arrived in PASS_ON:

            @pl.when(i == when[0] - (c // 2) * when[1] // (n_cube // 2))
            def _(arrived=arrived):
                pass_on(arrived)

        near_boxes_step(i, nb_s, q_ref, src_b, tgt_b, near_ref, lane, sub)
        return carry

    lax.fori_loop(0, boxes // BLOCK, near_step, 0)

    for i in range(n_oct - 1):
        to_oct(i).wait_recv()
    box = lax.broadcasted_iota(I32, (boxes, 2 * slots), 0).astype(F32)
    remote = None
    for m in range(n_oct // 4):
        hot, vals = [], []
        for e in (4 * m, 4 * m + 2):
            trow = got[e, slots : slots + 16, :].astype(F32) + got[
                e + 1, slots : slots + 16, :
            ].astype(F32)
            hot.append(jnp.where(box == trow[0:1], 1.0, 0.0).astype(BF16))
            vals += [got[e, 0:slots, :], got[e + 1, 0:slots, :]]
        part = jnp.dot(
            jnp.concatenate(hot, axis=1),
            jnp.concatenate(vals, axis=0),
            preferred_element_type=F32,
        )
        remote = part if remote is None else remote + part
    remote_ref[...] = remote

    widen(0, False)
    for n, off in enumerate(brought + [0]):
        to_sib[n].wait_recv()
        widen(off, True)

    def gather(blk, rows_ref, ks):
        for k in ks:
            for u in range(BLOCK):
                for e, at in enumerate(halves(gs_s[blk, k, u])):
                    place = (k + e * klist // 2) * BLOCK + u
                    rows_ref[place : place + 1, :] = gf_ref[pl.ds(at, 1), :]

    def pattern_sums(blk, vals, ps):
        t0 = pl.ds(pl.multiple_of(blk * BLOCK, BLOCK), BLOCK)
        total = jnp.dot(hot_ref[blk, BLOCK * ps[0] : BLOCK * (ps[-1] + 1), :], vals, preferred_element_type=F32)
        for n, p in enumerate(ps):
            sums_ref[t0, p * width : (p + 1) * width] = total[BLOCK * n : BLOCK * (n + 1)].astype(
                BF16
            )

    def both(nxt, nxt_ref, now, now_ref):
        vals = now_ref[...].astype(BF16)
        for k in range(klist // 2):
            gather(nxt, nxt_ref, (k,))
            pattern_sums(now, vals, tuple(range(2 * k * n_pat // klist, 2 * (k + 1) * n_pat // klist)))

    blocks = boxes // BLOCK
    gather(0, rows_a, range(klist // 2))

    def two_blocks(i, carry):
        both(2 * i + 1, rows_b, 2 * i, rows_a)
        both(jnp.minimum(2 * i + 2, blocks - 1), rows_a, 2 * i + 1, rows_b)
        return carry

    lax.fori_loop(0, blocks // 2, two_blocks, 0)
    operators = trans_ref[...].reshape(n_pat * width, width)
    local = jnp.dot(sums_ref[...], operators, preferred_element_type=F32) + remote_ref[...]

    far = jnp.dot(local.astype(BF16), eval_ref[...], preferred_element_type=F32)
    total = near_ref[...] * (1.0 / (4.0 * math.pi)) + far
    panel = lax.broadcasted_iota(I32, (boxes, panels), 1)
    out_ref[...] = jnp.where(panel < count_b[...], total, 0.0)

    for copy in to_chip + to_sib:
        copy.wait_send()
    for i in range(n_oct - 1):
        to_oct(i).wait_send()


def body(
    n_oct,
    n_cube,
    charges,
    panel_counts,
    positions,
    moment_map,
    translations,
    evaluation,
    near_boxes,
    group_sources,
    group_patterns,
    remote_sources,
    remote_patterns,
    remote_targets,
):
    boxes, panels = charges.shape
    width = moment_map.shape[1]
    n_pat = translations.shape[0]
    klist = group_sources.shape[1]
    slots, fanin = remote_sources.shape[3:]
    chips = n_cube // 2
    sources = remote_sources[0, 0].transpose(0, 2, 1)
    patterns = remote_patterns[0, 0].transpose(0, 2, 1)
    dma = pltpu.SemaphoreType.DMA
    return pl.pallas_call(
        functools.partial(step_kernel, n_oct, n_cube),
        out_shape=jax.ShapeDtypeStruct((boxes, panels), F32),
        in_specs=[pl.BlockSpec(memory_space=pltpu.HBM)] * 12,
        out_specs=pl.BlockSpec(memory_space=pltpu.VMEM),
        scratch_shapes=[
            pltpu.VMEM((boxes, panels), BF16),
            pltpu.VMEM((boxes // 128, 128), I32),
            pltpu.VMEM((panels, width), BF16),
            pltpu.VMEM((n_pat, width, width), BF16),
            pltpu.VMEM((n_oct, fanin, slots), I32),
            pltpu.VMEM((n_oct, fanin, slots), I32),
            pltpu.VMEM((near_boxes.shape[1], boxes), I32),
            pltpu.VMEM((n_oct, slots), I32),
            pltpu.VMEM((klist, boxes), I32),
            pltpu.VMEM((klist, boxes), I32),
            pltpu.VMEM((width, panels), BF16),
            pltpu.VMEM((boxes // BLOCK, 1, 128), I32),
            pltpu.SMEM((boxes // BLOCK, 1, 128), I32),
            pltpu.VMEM((boxes // BLOCK, klist // 2, 128), I32),
            pltpu.SMEM((boxes // BLOCK, klist // 2, 128), I32),
            pltpu.VMEM((boxes, 8, panels), F32),
            pltpu.VMEM((boxes, FEAT, panels), BF16),
            pltpu.VMEM((boxes // 4, panels, 4 * FEAT), BF16),
            pltpu.VMEM((boxes, panels), F32),
            pltpu.VMEM((boxes, panels), F32),
            pltpu.VMEM((boxes, panels), I32),
            pltpu.VMEM((n_cube, boxes, width), BF16),
            pltpu.VMEM((n_cube * boxes, width), F32),
            pltpu.VMEM((n_pat * boxes, width), F32),
            pltpu.VMEM((n_oct, fanin // 2, slots), I32),
            pltpu.SMEM((n_oct, fanin // 2, slots), I32),
            pltpu.VMEM((slots, width), F32),
            pltpu.VMEM((n_oct, slots + 16, width), BF16),
            pltpu.VMEM((n_oct, slots + 16, width), BF16),
            pltpu.VMEM((klist * BLOCK, width), F32),
            pltpu.VMEM((klist * BLOCK, width), F32),
            pltpu.VMEM((boxes // BLOCK, n_pat * BLOCK, klist * BLOCK), BF16),
            pltpu.VMEM((boxes, n_pat * width), BF16),
            pltpu.VMEM((boxes, width), F32),
            dma((11,)),
            dma((6,)),
            dma((3,)),
            dma((chips,)),
            dma((chips,)),
            dma((chips,)),
            dma((chips,)),
            dma((n_oct,)),
            dma((n_oct,)),
        ],
        compiler_params=pltpu.CompilerParams(
            collective_id=0, has_side_effects=True, vmem_limit_bytes=62 << 20
        ),
    )(
        positions,
        charges,
        panel_counts.reshape(boxes // 128, 128),
        moment_map,
        translations,
        sources,
        patterns,
        near_boxes.T,
        remote_targets[0, 0],
        group_sources.T,
        group_patterns.T,
        evaluation,
    )


def solution(mesh):
    n_oct, n_cube = mesh.shape["oct"], mesh.shape["cube"]
    return jax.shard_map(
        functools.partial(body, n_oct, n_cube),
        mesh=mesh,
        in_specs=(
            P(("oct", "cube"), None),
            P(("oct", "cube")),
            P(None, ("oct", "cube"), None),
            P(),
            P(),
            P(),
            P(("oct", "cube"), None),
            P(("oct", "cube"), None),
            P(("oct", "cube"), None),
            P("oct", "cube", None, None, None),
            P("oct", "cube", None, None, None),
            P("oct", "cube", None, None),
        ),
        out_specs=P(("oct", "cube"), None),
        check_vma=False,
    )
```

```python
import functools
import math

import jax
import jax.numpy as jnp
from jax import lax
from jax.experimental import pallas as pl
from jax.experimental.pallas import tpu as pltpu
from jax.sharding import PartitionSpec as P

F32, BF16, I32 = jnp.float32, jnp.bfloat16, jnp.int32
MESH = pl.DeviceIdType.MESH
FEAT = 32
SOFT = 0.0025
BLOCK = 32
CHIP_SENDS = ((0, 2), (0, -2), (0, 1), (0, -1), (-2, 1), (-2, 2), (2, -1))
PASS_ON = (((5, 4), (0, 1, 2, 3), (7,)), ((7, 1), (4, 5, 6), (0, 1, 2, 3)))


def parts3(v):
    hi = v.astype(BF16).astype(F32)
    rest = v - hi
    mid = rest.astype(BF16).astype(F32)
    return hi, mid, rest - mid


def merge(a, b, first, shift, axis):
    return jnp.where(first, a, b) + pltpu.roll(jnp.where(first, b, a), shift, axis)


def halves(word):
    return word & 65535, lax.shift_right_logical(word, 16)


def column(row):
    return jnp.broadcast_to(row, (128, 128)).T


def features_of_four(i, p_ref, src_b, tgt_b, sub):
    is3, is7, lo3, lo4 = sub == 3, sub == 7, sub < 3, sub < 4
    pad = is3 | is7
    zero = jnp.zeros((8, 128), F32)
    cols = []
    for u in range(4):
        t = 4 * i + u
        v = jnp.where(pad, 0.0, p_ref[t] - 1.0)
        s = v * v
        s = s + pltpu.roll(s, 1, 0)
        n = s + pltpu.roll(s, 2, 0)
        w1, w2, w3 = parts3(jnp.where(pad, n, v))
        s0 = jnp.where(is7, 1.0, w1)
        s1 = jnp.where(is7, 1.0, w2)
        s2 = jnp.where(is7, 1.0, jnp.where(lo3, w1, w3))
        src_b[t] = jnp.concatenate([s0, s1, s2, zero], axis=0).astype(BF16)
        m1, m2, m3 = parts3(n + SOFT)
        y1, y2, y3 = -2.0 * w1, -2.0 * w2, -2.0 * w3
        base = jnp.where(is3, 1.0, jnp.where(lo4, y1, y2))
        t0 = jnp.where(is7, m1, base)
        t1 = jnp.where(is7, m2, base)
        t2 = jnp.where(is7, m3, jnp.where(is3, 1.0, jnp.where(lo4, y3, y1)))
        cols += [t0, t1, t2, zero]
    tgt_b[i] = jnp.concatenate(cols, axis=0).T.astype(BF16)


def near_boxes_step(i, nb_ref, q_ref, src_b, tgt_b, near_ref, lane, sub):
    t0 = pl.multiple_of(BLOCK * i, BLOCK)
    rows = []
    for u in range(BLOCK):
        lhs = tgt_b[(BLOCK // 4) * i + u // 4]
        lo = FEAT * (u % 4)
        acc = None
        word = nb_ref[i, 0, u]
        for pair in range(2):
            ids = [lax.shift_right_logical(word, 16 * pair + 8 * e) & 255 for e in range(2)]
            parts = [jnp.concatenate([src_b[s] for s in ids], axis=1)]
            if lo:
                parts.insert(0, jnp.zeros((lo, 256), BF16))
            if lo + FEAT < 128:
                parts.append(jnp.zeros((128 - FEAT - lo, 256), BF16))
            rhs = jnp.concatenate(parts, axis=0)
            inv = lax.rsqrt(jnp.dot(lhs, rhs, preferred_element_type=F32))
            for e in range(2):
                q = q_ref[pl.ds(ids[e], 1), :]
                term = inv[:, 128 * e : 128 * e + 128] * q
                acc = term if acc is None else acc + term
        row = None
        for g in range(16):
            total = jnp.sum(acc[8 * g : 8 * g + 8], axis=1, keepdims=True)
            x = jnp.where(lane == sub + 8 * g, total, 0.0)
            row = x if row is None else row + x
        rows.append(row)
    for b in range(BLOCK // 8):
        some = rows[8 * b : 8 * b + 8]
        shift = 1
        while len(some) > 1:
            first = (sub & shift) == 0
            some = [merge(some[2 * n], some[2 * n + 1], first, shift, 0) for n in range(len(some) // 2)]
            shift *= 2
        near_ref[pl.ds(t0 + 8 * b, 8), :] = some[0]


def step_kernel(
    n_oct,
    n_cube,
    pos_ref,
    charges_in,
    counts_in,
    moment_in,
    trans_in,
    rs_in,
    rp_in,
    nb_in,
    rt_in,
    gs_in,
    gp_in,
    eval_in,
    out_ref,
    charges_ref,
    counts_ref,
    moment_ref,
    trans_ref,
    rs_ref,
    rp_ref,
    nb_ref,
    rt_ref,
    gs_ref,
    gp_ref,
    eval_ref,
    nb_v,
    nb_s,
    gs_v,
    gs_s,
    p_ref,
    src_b,
    tgt_b,
    q_ref,
    near_ref,
    count_b,
    gall,
    gf_ref,
    table,
    key_v,
    key_s,
    slot_f,
    msg,
    got,
    rows_a,
    rows_b,
    hot_ref,
    sums_ref,
    remote_ref,
    in_sem,
    pos_sem,
    key_sem,
    chip_send,
    chip_recv,
    sib_send,
    sib_recv,
    oct_send,
    oct_recv,
):
    o = lax.axis_index("oct")
    c = lax.axis_index("cube")
    boxes, panels = charges_ref.shape
    width = moment_ref.shape[1]
    n_pat = trans_ref.shape[0]
    klist = gs_ref.shape[0]
    fanin = rs_ref.shape[1]
    slots = rs_ref.shape[2]
    sib = c + 1 - 2 * lax.rem(c, 2)

    pairs = (
        (charges_in, charges_ref),
        (counts_in, counts_ref),
        (moment_in, moment_ref),
        (rs_in, rs_ref),
        (rp_in, rp_ref),
        (trans_in, trans_ref),
        (nb_in, nb_ref),
        (rt_in, rt_ref),
        (gs_in, gs_ref),
        (gp_in, gp_ref),
        (eval_in, eval_ref),
    )
    copies = [pltpu.make_async_copy(a, b, in_sem.at[i]) for i, (a, b) in enumerate(pairs)]
    pos_copies = [
        pltpu.make_async_copy(pos_ref.at[d], p_ref.at[:, d + 4 * e], pos_sem.at[d + 3 * e])
        for d in range(3)
        for e in range(2)
    ]
    for copy in copies[:5] + pos_copies + copies[5:]:
        copy.start()

    barrier = pltpu.get_barrier_semaphore()
    dests = sorted({d % (n_cube // 2) for _, d in CHIP_SENDS} | {-d % (n_cube // 2) for _, d in CHIP_SENDS})
    for peer in [sib] + [lax.rem(c + 2 * d, n_cube) for d in dests]:
        pl.semaphore_signal(barrier, inc=1, device_id={"cube": peer}, device_id_type=MESH)
    for i in range(n_oct - 1):
        d = lax.rem(o + 1 + i, n_oct)
        pl.semaphore_signal(barrier, inc=1, device_id={"oct": d}, device_id_type=MESH)

    lane = lax.broadcasted_iota(I32, (8, 128), 1)
    sub = lax.broadcasted_iota(I32, (8, 128), 0)

    for copy in copies[:5]:
        copy.wait()
    key = rp_ref[...] * boxes + rs_ref[...]
    key_v[...] = key[:, : fanin // 2] + key[:, fanin // 2 :] * 65536
    key_copy = pltpu.make_async_copy(key_v, key_s, key_sem.at[0])
    key_copy.start()
    lane_big = lax.broadcasted_iota(I32, (128, 128), 1)
    for h in range(boxes // 128):
        half = slice(128 * h, 128 * h + 128)
        count_b[half] = column(counts_ref[h : h + 1, :])
        charge = charges_ref[half].astype(F32)
        q_ref[half] = jnp.where(lane_big < count_b[half], charge, 0.0)
    strength = q_ref[...].astype(BF16)
    multipole = jnp.dot(strength, moment_ref[...], preferred_element_type=F32).astype(BF16)
    gall[c] = multipole
    for copy in copies[5:]:
        copy.wait()
    index_copies = []
    def four_bytes(v):
        return v[0:1] + v[1:2] * 256 + v[2:3] * 65536 + v[3:4] * 16777216

    def two_halves(v):
        return v[: klist // 2] + v[klist // 2 :] * 65536

    lists = ((nb_ref, nb_v, nb_s, four_bytes), (gs_ref, gs_v, gs_s, two_halves))
    for n, (whole, cut, scalar, packed) in enumerate(lists):
        for h in range(boxes // 128):
            entries = whole[:, 128 * h : 128 * h + 128]
            for e in range(128 // BLOCK):
                turn = (128 - BLOCK * e) % 128
                mine = pltpu.roll(entries, turn, 1) if turn else entries
                cut[h * (128 // BLOCK) + e] = packed(mine)
        index_copies.append(pltpu.make_async_copy(cut, scalar, key_sem.at[1 + n]))
        index_copies[-1].start()
    for p in range(n_pat):
        table[p * boxes : (p + 1) * boxes] = jnp.dot(
            multipole, trans_ref[p], preferred_element_type=F32
        )
    for copy in pos_copies:
        copy.wait()

    targets = rt_ref[...].astype(F32)
    blank = jnp.zeros_like(targets)
    odd = lax.rem(o, 2)
    target_rows = jnp.where(
        odd == 0,
        jnp.concatenate([targets, blank], axis=1),
        jnp.concatenate([blank, targets], axis=1),
    )
    for d in range(n_oct):
        msg[d, slots : slots + 16, :] = jnp.broadcast_to(
            target_rows[d : d + 1], (16, 2 * slots)
        ).astype(BF16)
    key_copy.wait()
    for copy in index_copies:
        copy.wait()
    groups_each = boxes // (4 * n_oct)

    def one_group(d, carry):
        for j in range(slots):
            total = None
            for k in range(fanin // 2):
                for at in halves(key_s[d, k, j]):
                    row = table[pl.ds(at, 1), :]
                    total = row if total is None else total + row
            slot_f[j : j + 1, :] = total
        for u in range(groups_each):
            features_of_four(d * groups_each + u, p_ref, src_b, tgt_b, sub)
        msg[d, 0:slots, :] = slot_f[...].astype(BF16)
        return carry

    lax.fori_loop(0, n_oct, one_group, 0)
    def shard_at(off):
        return lax.rem(c + 2 * off + n_cube, n_cube)

    def send(off, peer, sends, recvs, n):
        shard = shard_at(off)
        return pltpu.make_async_remote_copy(
            src_ref=gall.at[shard],
            dst_ref=gall.at[shard],
            send_sem=sends.at[n],
            recv_sem=recvs.at[n],
            device_id={"cube": peer},
            device_id_type=MESH,
        )

    to_chip = [send(s, shard_at(d), chip_send, chip_recv, n) for n, (s, d) in enumerate(CHIP_SENDS)]
    turn = 1 - 2 * lax.rem(c // 2, 2)
    far = CHIP_SENDS.index((-2, 2))
    to_chip[far] = send(-2 * turn, shard_at(2 * turn), chip_send, chip_recv, far)
    brought = [s - d for s, d in CHIP_SENDS]
    to_sib = [send(s, sib, sib_send, sib_recv, n) for n, s in enumerate(brought + [0])]

    def widen(off, other):
        shard = shard_at(off)
        if other:
            shard = shard + 1 - 2 * lax.rem(c, 2)
        rows = pl.ds(pl.multiple_of(shard * boxes, boxes), boxes)
        gf_ref[rows, :] = gall[shard].astype(F32)

    def pass_on(arrived, from_sib):
        for n in arrived:
            to_chip[n].wait_recv()
            for m, (s, d) in enumerate(CHIP_SENDS):
                if s != 0 and s == brought[n] and m != far:
                    to_chip[m].start()
            if brought[n] == 2:
                to_chip[far].start()
            to_sib[n].start()
        for n in arrived:
            widen(brought[n], False)
        for n in from_sib:
            to_sib[n].wait_recv()
            widen((brought + [0])[n], True)

    def to_oct(i):
        d = lax.rem(o + 1 + i, n_oct)
        return pltpu.make_async_remote_copy(
            src_ref=msg.at[d],
            dst_ref=got.at[o],
            send_sem=oct_send.at[i],
            recv_sem=oct_recv.at[i],
            device_id={"oct": d},
            device_id_type=MESH,
        )

    got[o] = msg[o]

    def open_up():
        pl.semaphore_wait(barrier, 1 + len(dests) + n_oct - 1)
        for n, (s, d) in enumerate(CHIP_SENDS):
            if s == 0:
                to_chip[n].start()
        to_sib[-1].start()
        for i in range(n_oct - 1):
            to_oct(i).start()

    open_up()

    lane_row = lax.broadcasted_iota(I32, (1, 128), 1)
    lane_blk = lax.broadcasted_iota(I32, (BLOCK, 128), 1)
    own = lax.rem(lane_blk, BLOCK) == lax.broadcasted_iota(I32, (BLOCK, 128), 0)
    per = 128 // BLOCK
    for h in range(boxes // 128):
        entries = gp_ref[:, 128 * h : 128 * h + 128]
        turned = [entries] + [pltpu.roll(entries, BLOCK * s, 1) for s in range(1, per)]
        for e in range(per):
            for half in range(klist // per):
                row = None
                for j in range(per):
                    piece = turned[(j - e) % per][per * half + j : per * half + j + 1]
                    row = piece if row is None else jnp.where(lane_row // BLOCK == j, piece, row)
                wanted = jnp.where(own, row, -1)
                for p in range(n_pat):
                    hot_ref[per * h + e, BLOCK * p : BLOCK * (p + 1), 128 * half : 128 * half + 128] = (
                        jnp.where(wanted == p, 1.0, 0.0).astype(BF16)
                    )

    def near_step(i, carry):
        for when, arrived, from_sib in PASS_ON:

            @pl.when(i == when[0] - (c // 2) * when[1] // (n_cube // 2))
            def _(arrived=arrived, from_sib=from_sib):
                pass_on(arrived, from_sib)

        near_boxes_step(i, nb_s, q_ref, src_b, tgt_b, near_ref, lane, sub)
        return carry

    lax.fori_loop(0, boxes // BLOCK, near_step, 0)

    for i in range(n_oct - 1):
        to_oct(i).wait_recv()
    box = lax.broadcasted_iota(I32, (boxes, 2 * slots), 0).astype(F32)
    remote = None
    for m in range(n_oct // 4):
        hot, vals = [], []
        for e in (4 * m, 4 * m + 2):
            trow = got[e, slots : slots + 16, :].astype(F32) + got[
                e + 1, slots : slots + 16, :
            ].astype(F32)
            hot.append(jnp.where(box == trow[0:1], 1.0, 0.0).astype(BF16))
            vals += [got[e, 0:slots, :], got[e + 1, 0:slots, :]]
        part = jnp.dot(
            jnp.concatenate(hot, axis=1),
            jnp.concatenate(vals, axis=0),
            preferred_element_type=F32,
        )
        remote = part if remote is None else remote + part
    remote_ref[...] = remote

    widen(0, False)
    for n, off in enumerate(brought + [0]):
        if n not in PASS_ON[0][2] + PASS_ON[1][2]:
            to_sib[n].wait_recv()
            widen(off, True)

    def gather(blk, rows_ref, ks):
        for k in ks:
            for u in range(BLOCK):
                for e, at in enumerate(halves(gs_s[blk, k, u])):
                    place = (k + e * klist // 2) * BLOCK + u
                    rows_ref[place : place + 1, :] = gf_ref[pl.ds(at, 1), :]

    def pattern_sums(blk, vals, ps):
        t0 = pl.ds(pl.multiple_of(blk * BLOCK, BLOCK), BLOCK)
        total = jnp.dot(hot_ref[blk, BLOCK * ps[0] : BLOCK * (ps[-1] + 1), :], vals, preferred_element_type=F32)
        for n, p in enumerate(ps):
            sums_ref[t0, p * width : (p + 1) * width] = total[BLOCK * n : BLOCK * (n + 1)].astype(
                BF16
            )

    def both(nxt, nxt_ref, now, now_ref):
        vals = now_ref[...].astype(BF16)
        for k in range(klist // 2):
            gather(nxt, nxt_ref, (k,))
            pattern_sums(now, vals, tuple(range(2 * k * n_pat // klist, 2 * (k + 1) * n_pat // klist)))

    blocks = boxes // BLOCK
    gather(0, rows_a, range(klist // 2))

    def two_blocks(i, carry):
        both(2 * i + 1, rows_b, 2 * i, rows_a)
        both(jnp.minimum(2 * i + 2, blocks - 1), rows_a, 2 * i + 1, rows_b)
        return carry

    lax.fori_loop(0, blocks // 2, two_blocks, 0)
    operators = trans_ref[...].reshape(n_pat * width, width)
    local = jnp.dot(sums_ref[...], operators, preferred_element_type=F32) + remote_ref[...]

    far_field = jnp.dot(local.astype(BF16), eval_ref[...], preferred_element_type=F32)
    total = near_ref[...] * (1.0 / (4.0 * math.pi)) + far_field
    panel = lax.broadcasted_iota(I32, (boxes, panels), 1)
    out_ref[...] = jnp.where(panel < count_b[...], total, 0.0)

    for copy in to_chip + to_sib:
        copy.wait_send()
    for i in range(n_oct - 1):
        to_oct(i).wait_send()


def body(
    n_oct,
    n_cube,
    charges,
    panel_counts,
    positions,
    moment_map,
    translations,
    evaluation,
    near_boxes,
    group_sources,
    group_patterns,
    remote_sources,
    remote_patterns,
    remote_targets,
):
    boxes, panels = charges.shape
    width = moment_map.shape[1]
    n_pat = translations.shape[0]
    klist = group_sources.shape[1]
    slots, fanin = remote_sources.shape[3:]
    chips = n_cube // 2
    sources = remote_sources[0, 0].transpose(0, 2, 1)
    patterns = remote_patterns[0, 0].transpose(0, 2, 1)
    dma = pltpu.SemaphoreType.DMA
    return pl.pallas_call(
        functools.partial(step_kernel, n_oct, n_cube),
        out_shape=jax.ShapeDtypeStruct((boxes, panels), F32),
        in_specs=[pl.BlockSpec(memory_space=pltpu.HBM)] * 12,
        out_specs=pl.BlockSpec(memory_space=pltpu.VMEM),
        scratch_shapes=[
            pltpu.VMEM((boxes, panels), BF16),
            pltpu.VMEM((boxes // 128, 128), I32),
            pltpu.VMEM((panels, width), BF16),
            pltpu.VMEM((n_pat, width, width), BF16),
            pltpu.VMEM((n_oct, fanin, slots), I32),
            pltpu.VMEM((n_oct, fanin, slots), I32),
            pltpu.VMEM((near_boxes.shape[1], boxes), I32),
            pltpu.VMEM((n_oct, slots), I32),
            pltpu.VMEM((klist, boxes), I32),
            pltpu.VMEM((klist, boxes), I32),
            pltpu.VMEM((width, panels), BF16),
            pltpu.VMEM((boxes // BLOCK, 1, 128), I32),
            pltpu.SMEM((boxes // BLOCK, 1, 128), I32),
            pltpu.VMEM((boxes // BLOCK, klist // 2, 128), I32),
            pltpu.SMEM((boxes // BLOCK, klist // 2, 128), I32),
            pltpu.VMEM((boxes, 8, panels), F32),
            pltpu.VMEM((boxes, FEAT, panels), BF16),
            pltpu.VMEM((boxes // 4, panels, 4 * FEAT), BF16),
            pltpu.VMEM((boxes, panels), F32),
            pltpu.VMEM((boxes, panels), F32),
            pltpu.VMEM((boxes, panels), I32),
            pltpu.VMEM((n_cube, boxes, width), BF16),
            pltpu.VMEM((n_cube * boxes, width), F32),
            pltpu.VMEM((n_pat * boxes, width), F32),
            pltpu.VMEM((n_oct, fanin // 2, slots), I32),
            pltpu.SMEM((n_oct, fanin // 2, slots), I32),
            pltpu.VMEM((slots, width), F32),
            pltpu.VMEM((n_oct, slots + 16, width), BF16),
            pltpu.VMEM((n_oct, slots + 16, width), BF16),
            pltpu.VMEM((klist * BLOCK, width), F32),
            pltpu.VMEM((klist * BLOCK, width), F32),
            pltpu.VMEM((boxes // BLOCK, n_pat * BLOCK, klist * BLOCK), BF16),
            pltpu.VMEM((boxes, n_pat * width), BF16),
            pltpu.VMEM((boxes, width), F32),
            dma((11,)),
            dma((6,)),
            dma((3,)),
            dma((chips,)),
            dma((chips,)),
            dma((chips,)),
            dma((chips,)),
            dma((n_oct,)),
            dma((n_oct,)),
        ],
        compiler_params=pltpu.CompilerParams(
            collective_id=0, has_side_effects=True, vmem_limit_bytes=62 << 20
        ),
    )(
        positions,
        charges,
        panel_counts.reshape(boxes // 128, 128),
        moment_map,
        translations,
        sources,
        patterns,
        near_boxes.T,
        remote_targets[0, 0],
        group_sources.T,
        group_patterns.T,
        evaluation,
    )


def solution(mesh):
    n_oct, n_cube = mesh.shape["oct"], mesh.shape["cube"]
    return jax.shard_map(
        functools.partial(body, n_oct, n_cube),
        mesh=mesh,
        in_specs=(
            P(("oct", "cube"), None),
            P(("oct", "cube")),
            P(None, ("oct", "cube"), None),
            P(),
            P(),
            P(),
            P(("oct", "cube"), None),
            P(("oct", "cube"), None),
            P(("oct", "cube"), None),
            P("oct", "cube", None, None, None),
            P("oct", "cube", None, None, None),
            P("oct", "cube", None, None),
        ),
        out_specs=P(("oct", "cube"), None),
        check_vma=False,
    )
```

```python
import functools
import math

import jax
import jax.numpy as jnp
from jax import lax
from jax.experimental import pallas as pl
from jax.experimental.pallas import tpu as pltpu
from jax.sharding import PartitionSpec as P

F32, BF16, I32 = jnp.float32, jnp.bfloat16, jnp.int32
MESH = pl.DeviceIdType.MESH
FEAT = 32
SOFT = 0.0025
BLOCK = 32
CHIP_SENDS = ((0, 2), (0, -2), (0, 1), (0, -1), (-2, 1), (-2, 2), (2, -1))
PASS_ON = (((5, 4), (0, 1, 2, 3), (7,)), ((7, 1), (4, 5, 6), (0, 1, 2, 3)))


def parts3(v):
    hi = v.astype(BF16).astype(F32)
    rest = v - hi
    mid = rest.astype(BF16).astype(F32)
    return hi, mid, rest - mid


def merge(a, b, first, shift, axis):
    return jnp.where(first, a, b) + pltpu.roll(jnp.where(first, b, a), shift, axis)


def halves(word):
    return word & 65535, lax.shift_right_logical(word, 16)


def column(row):
    return jnp.broadcast_to(row, (128, 128)).T


def features_of_four(i, p_ref, src_b, tgt_b, sub):
    is3, is7, lo3, lo4 = sub == 3, sub == 7, sub < 3, sub < 4
    pad = is3 | is7
    zero = jnp.zeros((8, 128), F32)
    cols = []
    for u in range(4):
        t = 4 * i + u
        v = jnp.where(pad, 0.0, p_ref[t] - 1.0)
        s = v * v
        s = s + pltpu.roll(s, 1, 0)
        n = s + pltpu.roll(s, 2, 0)
        w1, w2, w3 = parts3(jnp.where(pad, n, v))
        s0 = jnp.where(is7, 1.0, w1)
        s1 = jnp.where(is7, 1.0, w2)
        s2 = jnp.where(is7, 1.0, jnp.where(lo3, w1, w3))
        src_b[t] = jnp.concatenate([s0, s1, s2, zero], axis=0).astype(BF16)
        m1, m2, m3 = parts3(n + SOFT)
        y1, y2, y3 = -2.0 * w1, -2.0 * w2, -2.0 * w3
        base = jnp.where(is3, 1.0, jnp.where(lo4, y1, y2))
        t0 = jnp.where(is7, m1, base)
        t1 = jnp.where(is7, m2, base)
        t2 = jnp.where(is7, m3, jnp.where(is3, 1.0, jnp.where(lo4, y3, y1)))
        cols += [t0, t1, t2, zero]
    tgt_b[i] = jnp.concatenate(cols, axis=0).T.astype(BF16)


def near_boxes_step(i, nb_ref, q_ref, src_b, tgt_b, near_ref, lane, sub):
    t0 = pl.multiple_of(BLOCK * i, BLOCK)
    rows = []
    for u in range(BLOCK):
        lhs = tgt_b[(BLOCK // 4) * i + u // 4]
        lo = FEAT * (u % 4)
        acc = None
        word = nb_ref[i, 0, u]
        for pair in range(2):
            ids = [lax.shift_right_logical(word, 16 * pair + 8 * e) & 255 for e in range(2)]
            parts = [jnp.concatenate([src_b[s] for s in ids], axis=1)]
            if lo:
                parts.insert(0, jnp.zeros((lo, 256), BF16))
            if lo + FEAT < 128:
                parts.append(jnp.zeros((128 - FEAT - lo, 256), BF16))
            rhs = jnp.concatenate(parts, axis=0)
            inv = lax.rsqrt(jnp.dot(lhs, rhs, preferred_element_type=F32))
            for e in range(2):
                q = q_ref[pl.ds(ids[e], 1), :]
                term = inv[:, 128 * e : 128 * e + 128] * q
                acc = term if acc is None else acc + term
        row = None
        for g in range(16):
            total = jnp.sum(acc[8 * g : 8 * g + 8], axis=1, keepdims=True)
            x = jnp.where(lane == sub + 8 * g, total, 0.0)
            row = x if row is None else row + x
        rows.append(row)
    for b in range(BLOCK // 8):
        some = rows[8 * b : 8 * b + 8]
        shift = 1
        while len(some) > 1:
            first = (sub & shift) == 0
            some = [merge(some[2 * n], some[2 * n + 1], first, shift, 0) for n in range(len(some) // 2)]
            shift *= 2
        near_ref[pl.ds(t0 + 8 * b, 8), :] = some[0]


def step_kernel(
    n_oct,
    n_cube,
    pos_ref,
    charges_in,
    counts_in,
    moment_in,
    trans_in,
    rs_in,
    rp_in,
    nb_in,
    rt_in,
    gs_in,
    gp_in,
    eval_in,
    out_ref,
    charges_ref,
    counts_ref,
    moment_ref,
    trans_ref,
    rs_ref,
    rp_ref,
    nb_ref,
    rt_ref,
    gs_ref,
    gp_ref,
    eval_ref,
    nb_v,
    nb_s,
    gs_v,
    gs_s,
    p_ref,
    src_b,
    tgt_b,
    q_ref,
    near_ref,
    count_b,
    gall,
    gf_ref,
    table,
    key_v,
    key_s,
    slot_f,
    msg,
    got,
    rows_a,
    rows_b,
    hot_ref,
    sums_ref,
    remote_ref,
    in_sem,
    pos_sem,
    key_sem,
    chip_send,
    chip_recv,
    sib_send,
    sib_recv,
    oct_send,
    oct_recv,
):
    o = lax.axis_index("oct")
    c = lax.axis_index("cube")
    boxes, panels = charges_ref.shape
    width = moment_ref.shape[1]
    n_pat = trans_ref.shape[0]
    klist = gs_ref.shape[0]
    fanin = rs_ref.shape[1]
    slots = rs_ref.shape[2]
    sib = c + 1 - 2 * lax.rem(c, 2)

    pairs = (
        (charges_in, charges_ref),
        (counts_in, counts_ref),
        (moment_in, moment_ref),
        (rs_in, rs_ref),
        (rp_in, rp_ref),
        (trans_in, trans_ref),
        (nb_in, nb_ref),
        (rt_in, rt_ref),
        (gs_in, gs_ref),
        (gp_in, gp_ref),
        (eval_in, eval_ref),
    )
    copies = [pltpu.make_async_copy(a, b, in_sem.at[i]) for i, (a, b) in enumerate(pairs)]
    pos_copies = [
        pltpu.make_async_copy(pos_ref.at[d], p_ref.at[:, d + 4 * e], pos_sem.at[d + 3 * e])
        for d in range(3)
        for e in range(2)
    ]
    for copy in copies[:5] + pos_copies + copies[5:]:
        copy.start()

    barrier = pltpu.get_barrier_semaphore()
    dests = sorted({d % (n_cube // 2) for _, d in CHIP_SENDS} | {-d % (n_cube // 2) for _, d in CHIP_SENDS})
    for peer in [sib] + [lax.rem(c + 2 * d, n_cube) for d in dests]:
        pl.semaphore_signal(barrier, inc=1, device_id={"cube": peer}, device_id_type=MESH)
    for i in range(n_oct - 1):
        d = lax.rem(o + 1 + i, n_oct)
        pl.semaphore_signal(barrier, inc=1, device_id={"oct": d}, device_id_type=MESH)

    lane = lax.broadcasted_iota(I32, (8, 128), 1)
    sub = lax.broadcasted_iota(I32, (8, 128), 0)

    for copy in copies[:5]:
        copy.wait()
    key = rp_ref[...] * boxes + rs_ref[...]
    key_v[...] = key[:, : fanin // 2] + key[:, fanin // 2 :] * 65536
    key_copy = pltpu.make_async_copy(key_v, key_s, key_sem.at[0])
    key_copy.start()
    lane_big = lax.broadcasted_iota(I32, (128, 128), 1)
    for h in range(boxes // 128):
        half = slice(128 * h, 128 * h + 128)
        count_b[half] = column(counts_ref[h : h + 1, :])
        charge = charges_ref[half].astype(F32)
        q_ref[half] = jnp.where(lane_big < count_b[half], charge, 0.0)
    strength = q_ref[...].astype(BF16)
    multipole = jnp.dot(strength, moment_ref[...], preferred_element_type=F32).astype(BF16)
    gall[c] = multipole
    for copy in copies[5:]:
        copy.wait()
    for p in range(n_pat):
        table[p * boxes : (p + 1) * boxes] = jnp.dot(
            multipole, trans_ref[p], preferred_element_type=F32
        )
    for copy in pos_copies:
        copy.wait()

    targets = rt_ref[...].astype(F32)
    blank = jnp.zeros_like(targets)
    odd = lax.rem(o, 2)
    target_rows = jnp.where(
        odd == 0,
        jnp.concatenate([targets, blank], axis=1),
        jnp.concatenate([blank, targets], axis=1),
    )
    for d in range(n_oct):
        msg[d, slots : slots + 16, :] = jnp.broadcast_to(
            target_rows[d : d + 1], (16, 2 * slots)
        ).astype(BF16)
    key_copy.wait()
    groups_each = boxes // (4 * n_oct)

    def one_group(d, carry):
        for j in range(slots):
            total = None
            for k in range(fanin // 2):
                for at in halves(key_s[d, k, j]):
                    row = table[pl.ds(at, 1), :]
                    total = row if total is None else total + row
            slot_f[j : j + 1, :] = total
        for u in range(groups_each):
            features_of_four(d * groups_each + u, p_ref, src_b, tgt_b, sub)
        msg[d, 0:slots, :] = slot_f[...].astype(BF16)
        return carry

    lax.fori_loop(0, n_oct, one_group, 0)
    def shard_at(off):
        return lax.rem(c + 2 * off + n_cube, n_cube)

    def send(off, peer, sends, recvs, n):
        shard = shard_at(off)
        return pltpu.make_async_remote_copy(
            src_ref=gall.at[shard],
            dst_ref=gall.at[shard],
            send_sem=sends.at[n],
            recv_sem=recvs.at[n],
            device_id={"cube": peer},
            device_id_type=MESH,
        )

    to_chip = [send(s, shard_at(d), chip_send, chip_recv, n) for n, (s, d) in enumerate(CHIP_SENDS)]
    turn = 1 - 2 * lax.rem(c // 2, 2)
    far = CHIP_SENDS.index((-2, 2))
    to_chip[far] = send(-2 * turn, shard_at(2 * turn), chip_send, chip_recv, far)
    brought = [s - d for s, d in CHIP_SENDS]
    to_sib = [send(s, sib, sib_send, sib_recv, n) for n, s in enumerate(brought + [0])]

    def widen(off, other):
        shard = shard_at(off)
        if other:
            shard = shard + 1 - 2 * lax.rem(c, 2)
        rows = pl.ds(pl.multiple_of(shard * boxes, boxes), boxes)
        gf_ref[rows, :] = gall[shard].astype(F32)

    def pass_on(arrived, from_sib):
        for n in arrived:
            to_chip[n].wait_recv()
            for m, (s, d) in enumerate(CHIP_SENDS):
                if s != 0 and s == brought[n] and m != far:
                    to_chip[m].start()
            if brought[n] == 2:
                to_chip[far].start()
            to_sib[n].start()
        for n in arrived:
            widen(brought[n], False)
        for n in from_sib:
            to_sib[n].wait_recv()
            widen((brought + [0])[n], True)

    def to_oct(i):
        d = lax.rem(o + 1 + i, n_oct)
        return pltpu.make_async_remote_copy(
            src_ref=msg.at[d],
            dst_ref=got.at[o],
            send_sem=oct_send.at[i],
            recv_sem=oct_recv.at[i],
            device_id={"oct": d},
            device_id_type=MESH,
        )


    def open_up():
        pl.semaphore_wait(barrier, 1 + len(dests) + n_oct - 1)
        for n, (s, d) in enumerate(CHIP_SENDS):
            if s == 0:
                to_chip[n].start()
        to_sib[-1].start()
        for i in range(n_oct - 1):
            to_oct(i).start()

    open_up()
    got[o] = msg[o]

    index_copies = []
    def four_bytes(v):
        return v[0:1] + v[1:2] * 256 + v[2:3] * 65536 + v[3:4] * 16777216

    def two_halves(v):
        return v[: klist // 2] + v[klist // 2 :] * 65536

    lists = ((nb_ref, nb_v, nb_s, four_bytes), (gs_ref, gs_v, gs_s, two_halves))
    for n, (whole, cut, scalar, packed) in enumerate(lists):
        for h in range(boxes // 128):
            entries = whole[:, 128 * h : 128 * h + 128]
            for e in range(128 // BLOCK):
                turn = (128 - BLOCK * e) % 128
                mine = pltpu.roll(entries, turn, 1) if turn else entries
                cut[h * (128 // BLOCK) + e] = packed(mine)
        index_copies.append(pltpu.make_async_copy(cut, scalar, key_sem.at[1 + n]))
        index_copies[-1].start()

    lane_row = lax.broadcasted_iota(I32, (1, 128), 1)
    lane_blk = lax.broadcasted_iota(I32, (BLOCK, 128), 1)
    own = lax.rem(lane_blk, BLOCK) == lax.broadcasted_iota(I32, (BLOCK, 128), 0)
    per = 128 // BLOCK
    for h in range(boxes // 128):
        entries = gp_ref[:, 128 * h : 128 * h + 128]
        turned = [entries] + [pltpu.roll(entries, BLOCK * s, 1) for s in range(1, per)]
        for e in range(per):
            for half in range(klist // per):
                row = None
                for j in range(per):
                    piece = turned[(j - e) % per][per * half + j : per * half + j + 1]
                    row = piece if row is None else jnp.where(lane_row // BLOCK == j, piece, row)
                wanted = jnp.where(own, row, -1)
                for p in range(n_pat):
                    hot_ref[per * h + e, BLOCK * p : BLOCK * (p + 1), 128 * half : 128 * half + 128] = (
                        jnp.where(wanted == p, 1.0, 0.0).astype(BF16)
                    )

    for copy in index_copies:
        copy.wait()

    def near_step(i, carry):
        for when, arrived, from_sib in PASS_ON:

            @pl.when(i == when[0] - (c // 2) * when[1] // (n_cube // 2))
            def _(arrived=arrived, from_sib=from_sib):
                pass_on(arrived, from_sib)

        near_boxes_step(i, nb_s, q_ref, src_b, tgt_b, near_ref, lane, sub)
        return carry

    lax.fori_loop(0, boxes // BLOCK, near_step, 0)

    for i in range(n_oct - 1):
        to_oct(i).wait_recv()
    box = lax.broadcasted_iota(I32, (boxes, 2 * slots), 0).astype(F32)
    remote = None
    for m in range(n_oct // 4):
        hot, vals = [], []
        for e in (4 * m, 4 * m + 2):
            trow = got[e, slots : slots + 16, :].astype(F32) + got[
                e + 1, slots : slots + 16, :
            ].astype(F32)
            hot.append(jnp.where(box == trow[0:1], 1.0, 0.0).astype(BF16))
            vals += [got[e, 0:slots, :], got[e + 1, 0:slots, :]]
        part = jnp.dot(
            jnp.concatenate(hot, axis=1),
            jnp.concatenate(vals, axis=0),
            preferred_element_type=F32,
        )
        remote = part if remote is None else remote + part
    remote_ref[...] = remote

    widen(0, False)
    for n, off in enumerate(brought + [0]):
        if n not in PASS_ON[0][2] + PASS_ON[1][2]:
            to_sib[n].wait_recv()
            widen(off, True)

    def gather(blk, rows_ref, ks):
        for k in ks:
            for u in range(BLOCK):
                for e, at in enumerate(halves(gs_s[blk, k, u])):
                    place = (k + e * klist // 2) * BLOCK + u
                    rows_ref[place : place + 1, :] = gf_ref[pl.ds(at, 1), :]

    def pattern_sums(blk, vals, ps):
        t0 = pl.ds(pl.multiple_of(blk * BLOCK, BLOCK), BLOCK)
        total = jnp.dot(hot_ref[blk, BLOCK * ps[0] : BLOCK * (ps[-1] + 1), :], vals, preferred_element_type=F32)
        for n, p in enumerate(ps):
            sums_ref[t0, p * width : (p + 1) * width] = total[BLOCK * n : BLOCK * (n + 1)].astype(
                BF16
            )

    def both(nxt, nxt_ref, now, now_ref):
        vals = now_ref[...].astype(BF16)
        for k in range(klist // 2):
            gather(nxt, nxt_ref, (k,))
            pattern_sums(now, vals, tuple(range(2 * k * n_pat // klist, 2 * (k + 1) * n_pat // klist)))

    blocks = boxes // BLOCK
    gather(0, rows_a, range(klist // 2))

    def two_blocks(i, carry):
        both(2 * i + 1, rows_b, 2 * i, rows_a)
        both(jnp.minimum(2 * i + 2, blocks - 1), rows_a, 2 * i + 1, rows_b)
        return carry

    lax.fori_loop(0, blocks // 2, two_blocks, 0)
    operators = trans_ref[...].reshape(n_pat * width, width)
    local = jnp.dot(sums_ref[...], operators, preferred_element_type=F32) + remote_ref[...]

    far_field = jnp.dot(local.astype(BF16), eval_ref[...], preferred_element_type=F32)
    total = near_ref[...] * (1.0 / (4.0 * math.pi)) + far_field
    panel = lax.broadcasted_iota(I32, (boxes, panels), 1)
    out_ref[...] = jnp.where(panel < count_b[...], total, 0.0)

    for copy in to_chip + to_sib:
        copy.wait_send()
    for i in range(n_oct - 1):
        to_oct(i).wait_send()


def body(
    n_oct,
    n_cube,
    charges,
    panel_counts,
    positions,
    moment_map,
    translations,
    evaluation,
    near_boxes,
    group_sources,
    group_patterns,
    remote_sources,
    remote_patterns,
    remote_targets,
):
    boxes, panels = charges.shape
    width = moment_map.shape[1]
    n_pat = translations.shape[0]
    klist = group_sources.shape[1]
    slots, fanin = remote_sources.shape[3:]
    chips = n_cube // 2
    sources = remote_sources[0, 0].transpose(0, 2, 1)
    patterns = remote_patterns[0, 0].transpose(0, 2, 1)
    dma = pltpu.SemaphoreType.DMA
    return pl.pallas_call(
        functools.partial(step_kernel, n_oct, n_cube),
        out_shape=jax.ShapeDtypeStruct((boxes, panels), F32),
        in_specs=[pl.BlockSpec(memory_space=pltpu.HBM)] * 12,
        out_specs=pl.BlockSpec(memory_space=pltpu.VMEM),
        scratch_shapes=[
            pltpu.VMEM((boxes, panels), BF16),
            pltpu.VMEM((boxes // 128, 128), I32),
            pltpu.VMEM((panels, width), BF16),
            pltpu.VMEM((n_pat, width, width), BF16),
            pltpu.VMEM((n_oct, fanin, slots), I32),
            pltpu.VMEM((n_oct, fanin, slots), I32),
            pltpu.VMEM((near_boxes.shape[1], boxes), I32),
            pltpu.VMEM((n_oct, slots), I32),
            pltpu.VMEM((klist, boxes), I32),
            pltpu.VMEM((klist, boxes), I32),
            pltpu.VMEM((width, panels), BF16),
            pltpu.VMEM((boxes // BLOCK, 1, 128), I32),
            pltpu.SMEM((boxes // BLOCK, 1, 128), I32),
            pltpu.VMEM((boxes // BLOCK, klist // 2, 128), I32),
            pltpu.SMEM((boxes // BLOCK, klist // 2, 128), I32),
            pltpu.VMEM((boxes, 8, panels), F32),
            pltpu.VMEM((boxes, FEAT, panels), BF16),
            pltpu.VMEM((boxes // 4, panels, 4 * FEAT), BF16),
            pltpu.VMEM((boxes, panels), F32),
            pltpu.VMEM((boxes, panels), F32),
            pltpu.VMEM((boxes, panels), I32),
            pltpu.VMEM((n_cube, boxes, width), BF16),
            pltpu.VMEM((n_cube * boxes, width), F32),
            pltpu.VMEM((n_pat * boxes, width), F32),
            pltpu.VMEM((n_oct, fanin // 2, slots), I32),
            pltpu.SMEM((n_oct, fanin // 2, slots), I32),
            pltpu.VMEM((slots, width), F32),
            pltpu.VMEM((n_oct, slots + 16, width), BF16),
            pltpu.VMEM((n_oct, slots + 16, width), BF16),
            pltpu.VMEM((klist * BLOCK, width), F32),
            pltpu.VMEM((klist * BLOCK, width), F32),
            pltpu.VMEM((boxes // BLOCK, n_pat * BLOCK, klist * BLOCK), BF16),
            pltpu.VMEM((boxes, n_pat * width), BF16),
            pltpu.VMEM((boxes, width), F32),
            dma((11,)),
            dma((6,)),
            dma((3,)),
            dma((chips,)),
            dma((chips,)),
            dma((chips,)),
            dma((chips,)),
            dma((n_oct,)),
            dma((n_oct,)),
        ],
        compiler_params=pltpu.CompilerParams(
            collective_id=0, has_side_effects=True, vmem_limit_bytes=62 << 20
        ),
    )(
        positions,
        charges,
        panel_counts.reshape(boxes // 128, 128),
        moment_map,
        translations,
        sources,
        patterns,
        near_boxes.T,
        remote_targets[0, 0],
        group_sources.T,
        group_patterns.T,
        evaluation,
    )


def solution(mesh):
    n_oct, n_cube = mesh.shape["oct"], mesh.shape["cube"]
    return jax.shard_map(
        functools.partial(body, n_oct, n_cube),
        mesh=mesh,
        in_specs=(
            P(("oct", "cube"), None),
            P(("oct", "cube")),
            P(None, ("oct", "cube"), None),
            P(),
            P(),
            P(),
            P(("oct", "cube"), None),
            P(("oct", "cube"), None),
            P(("oct", "cube"), None),
            P("oct", "cube", None, None, None),
            P("oct", "cube", None, None, None),
            P("oct", "cube", None, None),
        ),
        out_specs=P(("oct", "cube"), None),
        check_vma=False,
    )
```
